32 devices in a mesh: lat: 8 (over z, y), grp: 4 (over x, core).
Axes of the slice: x: 2, y: 2, z: 4, core: 2. Of those that a mesh axis runs over, the one named last changes fastest.
Arguments:
- tokens: bfloat16 [384, 64, 1024], P('grp', 'lat'), may hold values from -6 to 6
- cotangent: bfloat16 [384, 64, 1024], P('grp', 'lat'), may hold values from -6 to 6
- gain: float32 [384], P('grp'), may hold values from 0.5 to 1.5
- shift: float32 [384], P('grp'), may hold values from -3 to 3
- w_in: float32 [4, 2, 96, 96], P('grp'), may hold values from -0.4375 to 0.4375
- b_in: float32 [4, 2, 96], P('grp'), may hold values from -0.3 to 0.3
- w_out: float32 [4, 2, 96, 96], P('grp'), may hold values from -0.4375 to 0.4375
- b_out: float32 [4, 2, 96], P('grp'), may hold values from -0.12 to 0.12
Outputs:
- mixed: bfloat16 [384, 64, 1024], P('grp', 'lat')
- grad_tokens: bfloat16 [384, 64, 1024], P('grp', 'lat')
- grad_weights: float32 [4, 36864], P('grp', 'lat')
The draws below stay inside these ranges and needn't reach their ends.
All inputs are finite; a program needn't handle non-finite values.
Results may differ from the reference program's by a relative error of at most 0.012.
Values sent between devices are 32-bit elements; how exact they have to be, the bound alone decides.
A program may use at most 128 MiB of HBM per device.

```python
import math
import jax
import jax.numpy as jnp
from jax import lax

BLOCK_SIZE = 96
LON = 1024
LAT_ROWS = 64
MODES = 512
BLOCKS = 4
WIDTH = 384


def block_levels(rng, dims, shards, low, high):
    factor_of = 1.0
    for axis_at, shards_of in shards:
        draws = jax.random.uniform(jax.random.fold_in(jax.random.fold_in(rng, 6), axis_at), (shards_of,), jnp.float32, low / len(shards), high / len(shards))
        factor_of = factor_of * jnp.repeat(jnp.exp(draws), dims[axis_at] // shards_of).reshape((-1,) + (1,) * (len(dims) - 1 - axis_at))
    return factor_of


def centred(own_key, dims, scale, limit, cuts=(), held_as=jnp.bfloat16):
    level = block_levels(own_key, dims, cuts, -0.22, 0.18) if cuts else 1.0
    values = jax.random.normal(own_key, dims, jnp.float32) * scale * level
    return jnp.minimum(jnp.maximum(values, -limit), limit).astype(held_as)


def setup_inputs(seed: int = 0) -> dict:
    streams_of = jax.random.split(jax.random.key(seed), 9)
    return {
        "tokens": centred(streams_of[0], (WIDTH, LAT_ROWS, LON), 1.0, 6.0, ((0, 4), (1, 8))),
        "cotangent": centred(streams_of[1], (WIDTH, LAT_ROWS, LON), 1.0, 6.0, ((0, 4), (1, 8))),
        "gain": jnp.clip(1.0 + 0.1 * jax.random.normal(streams_of[2], (WIDTH,), jnp.float32), 0.5, 1.5),
        "shift": centred(streams_of[3], (WIDTH,), 0.5, 3.0, ((0, 4),), jnp.float32),
        "w_in": centred(streams_of[4], (BLOCKS, 2, BLOCK_SIZE, BLOCK_SIZE), (2 * BLOCK_SIZE) ** -0.5, 0.4375, ((0, 4),), jnp.float32),
        "b_in": centred(streams_of[5], (BLOCKS, 2, BLOCK_SIZE), 0.05, 0.3, ((0, 4),), jnp.float32),
        "w_out": centred(streams_of[6], (BLOCKS, 2, BLOCK_SIZE, BLOCK_SIZE), (2 * BLOCK_SIZE) ** -0.5, 0.4375, ((0, 4),), jnp.float32),
        "b_out": centred(streams_of[7], (BLOCKS, 2, BLOCK_SIZE), 0.02, 0.12, ((0, 4),), jnp.float32),
    }


highest = lax.Precision.HIGHEST
shrink_level = 0.01
norm_eps = 1e-05

def complex_mix(left_real, left_imag, w_real, w_imag):
    form = 'ihk,io->ohk'
    out_real = jnp.einsum(form, left_real, w_real, precision=highest) - jnp.einsum(form, left_imag, w_imag, precision=highest)
    out_imag = jnp.einsum(form, left_imag, w_real, precision=highest) + jnp.einsum(form, left_real, w_imag, precision=highest)
    return (out_real, out_imag)

def shrink(value):
    return jnp.sign(value) * jnp.maximum(jnp.abs(value) - shrink_level, 0.0)

def spectral_filter(field, in_real, in_imag, out_real, out_imag, bias_in, bias_out):
    half = jnp.fft.rfft(field, axis=2, norm='ortho')[:, :, :MODES]
    spectrum = jnp.fft.fft(half, axis=1, norm='ortho')
    pre_real, pre_imag = complex_mix(jnp.real(spectrum), jnp.imag(spectrum), in_real, in_imag)
    act_real = jax.nn.relu(pre_real + bias_in[0][:, None, None])
    act_imag = jax.nn.relu(pre_imag + bias_in[1][:, None, None])
    post_real, post_imag = complex_mix(act_real, act_imag, out_real, out_imag)
    shrunk_real = shrink(post_real + bias_out[0][:, None, None])
    shrunk_imag = shrink(post_imag + bias_out[1][:, None, None])
    back = jnp.fft.ifft(lax.complex(shrunk_real, shrunk_imag), axis=1, norm='ortho')
    return jnp.fft.irfft(back, n=LON, axis=2, norm='ortho')

def per_block(items):
    field, grad_part, block_in, bias_in, block_out, bias_out = items

    def apply_filter(value, in_real, in_imag, out_real, out_imag):
        return spectral_filter(value, in_real, in_imag, out_real, out_imag, bias_in, bias_out)
    filtered, pullback = jax.vjp(apply_filter, field, block_in[0], block_in[1], block_out[0], block_out[1])
    d_field, g_in_real, g_in_imag, g_out_real, g_out_imag = pullback(grad_part)
    grads = jnp.stack([g_in_real, g_in_imag, g_out_real, g_out_imag]).reshape(-1)
    return (filtered, d_field, grads)

def reference(tokens, cotangent, gain, shift, w_in, b_in, w_out, b_out):
    tok_val = tokens.astype(jnp.float32)
    grad_val = cotangent.astype(jnp.float32)
    token_mean = lax.optimization_barrier(jnp.mean(tok_val, axis=0))
    square_mean = lax.optimization_barrier(jnp.mean(tok_val * tok_val, axis=0))
    inv_std = lax.rsqrt(square_mean - token_mean * token_mean + norm_eps)
    normed = (tok_val - token_mean) * inv_std
    normal_out = normed * gain[:, None, None] + shift[:, None, None]

    def shaped(value):
        return value.reshape(BLOCKS, BLOCK_SIZE, LAT_ROWS, LON)
    filtered, d_filter, grads = lax.map(per_block, (shaped(normal_out), shaped(grad_val), w_in, b_in, w_out, b_out))
    filtered = filtered.reshape(WIDTH, LAT_ROWS, LON)
    d_filter = d_filter.reshape(WIDTH, LAT_ROWS, LON)
    mixed = (filtered + normal_out + tok_val).astype(jnp.bfloat16)
    d_normal = grad_val + d_filter
    dnorm = d_normal * gain[:, None, None]
    back_one = lax.optimization_barrier(jnp.mean(dnorm, axis=0))
    back_two = lax.optimization_barrier(jnp.mean(dnorm * normed, axis=0))
    grad_tokens = (grad_val + inv_std * (dnorm - back_one - normed * back_two)).astype(jnp.bfloat16)
    grad_weights = grads * (1.0 / math.sqrt(LAT_ROWS * MODES))
    return (mixed, grad_tokens, grad_weights)
```

```python
import functools
import math

import numpy as np
import ml_dtypes
import jax
import jax.numpy as jnp
from jax import lax
from jax.experimental import pallas as pl
from jax.experimental.pallas import tpu as pltpu
from jax.sharding import PartitionSpec as P

shrink_level = 0.01
norm_eps = 1e-05


precise = lax.Precision.HIGH
exact = lax.Precision.HIGHEST


def contract(form, left, right, level=precise):
    return jnp.einsum(form, left, right, precision=level, preferred_element_type=jnp.float32)


def angles(left_count, right_count, length):
    phase = np.arange(left_count)[:, None] * np.arange(right_count)[None, :] % length
    theta = phase * (2.0 * math.pi / length)
    return np.cos(theta), np.sin(theta)


def lon_table(length, modes, owners):
    cos_tab, sin_tab = angles(length, modes, length)
    both = np.stack([cos_tab, -sin_tab]) / math.sqrt(length)
    both = both.reshape(2, length, owners, modes // owners)
    return both.transpose(1, 2, 0, 3).astype(np.float32)


def lat_table(length):
    cos_tab, sin_tab = angles(length, length, length)
    table = np.stack([np.stack([cos_tab, -sin_tab]), np.stack([sin_tab, cos_tab])])
    return (table / math.sqrt(length)).transpose(2, 0, 3, 1).astype(np.float32)


def group_sum(value, name):
    count = lax.axis_size(name)
    total = value
    for step in range(1, count):
        pairs = [(at, (at + step) % count) for at in range(count)]
        total = total + lax.ppermute(value, name, pairs)
    return total


def scatter_sum(pieces, name):
    count = lax.axis_size(name)
    own = lax.axis_index(name)
    total = lax.dynamic_slice_in_dim(pieces, own, 1, axis=0)
    for step in range(1, count):
        pairs = [(at, (at + step) % count) for at in range(count)]
        piece = lax.dynamic_slice_in_dim(pieces, (own + step) % count, 1, axis=0)
        total = total + lax.ppermute(piece, name, pairs)
    return total


def swap(value):
    return lax.all_to_all(value, "lat", split_axis=0, concat_axis=0, tiled=True)


def mix_matrix(weight):
    real_part, imag_part = weight[0], weight[1]
    top = jnp.stack([real_part, imag_part], axis=1)
    low = jnp.stack([-imag_part, real_part], axis=1)
    return jnp.stack([top, low])


def shrink(value):
    return jnp.sign(value) * jnp.maximum(jnp.abs(value) - shrink_level, 0.0)


def matrix_grad(full):
    real_part = full[0, :, 0] + full[1, :, 1]
    imag_part = full[0, :, 1] - full[1, :, 0]
    return real_part, imag_part


def per_device(tokens, cotangent, gain, shift, w_in, b_in, w_out, b_out):
    chans, rows, length = tokens.shape
    lat_count = lax.axis_size("lat")
    all_chans = chans * lax.axis_size("grp")
    modes = length // 2
    own = modes // lat_count
    lat_len = rows * lat_count
    table = lon_table(length, modes, lat_count).reshape(length, 2 * modes)
    table = jnp.asarray(table)
    lat_tab = jnp.asarray(lat_table(lat_len)).reshape(lat_count, rows, 2, lat_len, 2)
    tok_val = tokens.astype(jnp.float32)
    grad_val = cotangent.astype(jnp.float32)

    def lon_parts(field, level):
        out = contract("crn,ndq->dcrq", field, table.reshape(length, lat_count, 2 * own), level)
        return out.reshape(lat_count, chans * rows, 2 * own)

    def lat_in(parts, level):
        parts = parts.reshape(lat_count, chans, rows, 2, own)
        return contract("scrim,srikj->kmjc", parts, lat_tab, level)

    def lat_out(value):
        out = contract("kmjc,srikj->scrim", value, lat_tab)
        return out.reshape(lat_count, chans * rows, 2 * own)

    def lon_back(parts):
        parts = parts.reshape(lat_count, chans, rows, 2 * own)
        return contract("dcrq,ndq->crn", parts, table.reshape(length, lat_count, 2 * own))

    sums = jnp.stack([jnp.sum(tok_val, axis=0), jnp.sum(tok_val * tok_val, axis=0)])
    sums = group_sum(sums, "grp")
    token_mean = sums[0] / all_chans
    inv_std = lax.rsqrt(sums[1] / all_chans - token_mean * token_mean + norm_eps)
    normed = (tok_val - token_mean) * inv_std
    normal_out = normed * gain[:, None, None] + shift[:, None, None]
    send_field, grad_val = lax.optimization_barrier((lon_parts(normal_out, exact), grad_val))
    recv_field = swap(send_field)
    recv_grad = swap(lon_parts(grad_val, precise))

    mat_in, mat_out = mix_matrix(w_in[0]), mix_matrix(w_out[0])
    at_mode = lax.axis_index("lat") * own + jnp.arange(own)
    mode_weight = jnp.where(at_mode == 0, 1.0, 2.0).astype(jnp.float32)[None, :, None, None]
    spec = lat_in(recv_field, exact)
    pre = contract("kmic,icjo->kmjo", spec, mat_in, exact) + b_in[0]
    act = jax.nn.relu(pre)
    post = contract("kmic,icjo->kmjo", act, mat_out, exact) + b_out[0]
    back_field = lat_out(shrink(post) * mode_weight)
    back_field, spec, pre, act, post, recv_grad = lax.optimization_barrier(
        (back_field, spec, pre, act, post, recv_grad)
    )
    rows_field = swap(back_field)

    grad = lat_in(recv_grad, precise) * mode_weight
    d_post = jnp.where(jnp.abs(post) > shrink_level, grad, 0.0)
    d_act = contract("kmjo,icjo->kmic", d_post, mat_out)
    d_pre = jnp.where(pre > 0.0, d_act, 0.0)
    d_spec = contract("kmjo,icjo->kmic", d_pre, mat_in)
    back_grad, spec, act, d_post, d_pre = lax.optimization_barrier(
        (lat_out(d_spec), spec, act, d_post, d_pre)
    )
    rows_grad = swap(back_grad)
    full_out = contract("kmic,kmjo->icjo", act, d_post)
    full_in = contract("kmic,kmjo->icjo", spec, d_pre)
    grads = jnp.stack([*matrix_grad(full_in), *matrix_grad(full_out)])
    grads = grads.reshape(lat_count, -1) * (1.0 / math.sqrt(lat_len * modes))
    grad_weights = scatter_sum(grads, "lat")

    mixed = (lon_back(rows_field) + normal_out + tok_val).astype(jnp.bfloat16)
    dnorm = (grad_val + lon_back(rows_grad)) * gain[:, None, None]
    back = group_sum(jnp.stack([jnp.sum(dnorm, axis=0), jnp.sum(dnorm * normed, axis=0)]), "grp")
    grad_tokens = grad_val + inv_std * (
        dnorm - back[0] / all_chans - normed * (back[1] / all_chans)
    )
    return (mixed, grad_tokens.astype(jnp.bfloat16), grad_weights)


MESH = pl.DeviceIdType.MESH


def flip(value, half):
    return pltpu.roll(value, half, value.ndim - 1)


def rotate(value, step, count, sense, sign, half):
    step = step % count
    if step == 0:
        return value
    if 2 * step == count:
        return -value
    angle = sense * 2.0 * math.pi * step / count
    turned = sign * flip(value, half)
    if 4 * step == count or 4 * step == 3 * count:
        return turned if math.sin(angle) > 0 else -turned
    return value * math.cos(angle) + turned * math.sin(angle)


def butterflies(values, sense, sign, half):
    count = len(values)
    if count == 1:
        return values
    even = butterflies(values[0::2], sense, sign, half)
    odd = butterflies(values[1::2], sense, sign, half)
    low, high = [], []
    for at in range(count // 2):
        turned = rotate(odd[at], at, count, sense, sign, half)
        low.append(even[at] + turned)
        high.append(even[at] - turned)
    return low + high


def dot(left, right):
    return lax.dot_general(
        left, right, (((1,), (0,)), ((), ())), preferred_element_type=jnp.float32
    )


def dot_lanes(left, right):
    return lax.dot_general(
        left, right, (((1,), (1,)), ((), ())), preferred_element_type=jnp.float32
    )


def halves(value):
    high = value.astype(jnp.bfloat16)
    return high, (value - high.astype(jnp.float32)).astype(jnp.bfloat16)


def band_kernel(
    lat_count, grp_count,
    tok_hbm, cot_hbm, high_hbm, low_hbm, back_hbm, gain, shift, w_in, b_in, w_out, b_out,
    mixed_hbm, gtok_hbm, gw_out,
    tok, cot, high_tab, low_tab, back_tab, norm_high, norm_low,
    f1_send, f1_recv, f2_send, f2_recv, b1_send, b1_recv, b2_send, b2_recv,
    spec, act, shrunk, gspec, work, stats, sum_send, sum_recv,
    mix_in, mix_out, pull_in, pull_out, bias_in, bias_out, acc_in, acc_out,
    gw_send, gw_recv, send_sem, recv_sem, load_sem,
):
    me, grp = lax.axis_index("lat"), lax.axis_index("grp")
    modes_all, chans, lanes = spec.shape
    half = lanes // 2
    all_rows, length = tok.shape
    rows = all_rows // chans
    chunks = length // lanes
    all_chans = chans * grp_count
    group = 16 // rows if rows < 16 else 1
    tile = group * rows

    def partner(step):
        other, bit = me, 1
        while bit < lat_count:
            if step & bit:
                other = other + bit * (1 - 2 * lax.rem(lax.div(me, bit), 2))
            bit *= 2
        return other

    def send(src, dst, kind, step):
        copy = pltpu.make_async_remote_copy(
            src_ref=src, dst_ref=dst,
            send_sem=send_sem.at[kind * lat_count + step],
            recv_sem=recv_sem.at[kind * lat_count + step],
            device_id=(partner(step), grp), device_id_type=MESH,
        )
        copy.start()
        return copy

    def load(src, dst, at):
        copy = pltpu.make_async_copy(src, dst, load_sem.at[at])
        copy.start()
        return copy

    order = list(range(lat_count - 1, 0, -1))
    first = order[0]

    load_cot = load(cot_hbm, cot, 0)
    load_first = load(high_hbm.at[partner(first)], high_tab.at[partner(first)], 1)
    load_tok = load(tok_hbm, tok, 2)
    table_loads = {}
    for step in order[1:] + [0]:
        d = partner(step)
        table_loads[step] = load(high_hbm.at[d], high_tab.at[d], 8 + step)
    load_low = load(low_hbm, low_tab, 3)
    load_back = load(back_hbm, back_tab, 4)

    barrier = pltpu.get_barrier_semaphore()
    for step in range(1, lat_count):
        pl.semaphore_signal(barrier, inc=1, device_id=(partner(step), grp), device_id_type=MESH)
    for step in range(1, grp_count):
        pl.semaphore_signal(
            barrier, inc=1, device_id=(me, lax.rem(grp + step, grp_count)), device_id_type=MESH
        )

    lane = lax.broadcasted_iota(jnp.int32, (1, lanes), 1)
    real_lane = lane < half
    sign = jnp.where(real_lane, -1.0, 1.0).astype(jnp.float32)
    at_mode = jnp.where(real_lane, lane, lane - half) + me * half
    mode_weight = jnp.where(at_mode == 0, 1.0, 2.0).astype(jnp.float32)
    norm = 1.0 / math.sqrt(modes_all)

    def lon(dst, d, left_high, left_low):
        size = min(256, all_rows)

        def body(at, carry):
            part = pl.ds(pl.multiple_of(at * size, size), size)
            out = dot(left_high[part, :], high_tab[d])
            if left_low is not None:
                out = out + dot(left_low[part, :], high_tab[d])
                out = out + dot(left_high[part, :], low_tab[d])
            dst[part, :] = out
            return carry

        lax.fori_loop(0, all_rows // size, body, 0)

    def group_exchange(use):
        copies = []
        for step in range(1, grp_count):
            copy = pltpu.make_async_remote_copy(
                src_ref=sum_send.at[use], dst_ref=sum_recv.at[use, step],
                send_sem=send_sem.at[(5 + use) * lat_count + step],
                recv_sem=recv_sem.at[(5 + use) * lat_count + step],
                device_id=(me, lax.rem(grp + step, grp_count)), device_id_type=MESH,
            )
            copy.start()
            copies.append(copy)
        return copies

    def group_total(use, copies, at):
        for copy in copies:
            copy.wait_recv()
        total = sum_send[use, at]
        for step in range(1, grp_count):
            total = total + sum_recv[use, step, at]
        return total

    load_cot.wait()
    load_first.wait()
    lon(f2_send.at[partner(first)], partner(first), cot, None)
    pl.semaphore_wait(barrier, lat_count - 1 + grp_count - 1)
    f2 = {first: send(f2_send.at[partner(first)], f2_recv.at[me], 1, first)}

    load_tok.wait()

    def sums(at, carry):
        one, two = carry
        part = tok[pl.ds(pl.multiple_of(at * tile, tile), tile), :].astype(jnp.float32)
        for item in range(group):
            value = part[item * rows:(item + 1) * rows, :]
            one, two = one + value, two + value * value
        return one, two

    zero = jnp.zeros((rows, length), jnp.float32)
    one, two = lax.fori_loop(0, all_rows // tile, sums, (zero, zero))
    sum_send[0, 0], sum_send[0, 1] = one, two
    stat_copies = group_exchange(0)

    def prepare(weight, bias, mix, pull, bias_to):
        real_part, imag_part = weight[0, 0], weight[0, 1]
        forward = jnp.concatenate([real_part, imag_part], axis=0).T
        high, low = halves(forward)
        mix[:chans], mix[chans:] = high, low
        backward = jnp.concatenate([real_part.T, imag_part.T], axis=0).T
        high, low = halves(backward)
        pull[:chans], pull[chans:] = high, low
        wide_real = jnp.broadcast_to(bias[0, 0:1, :], (lanes, chans)).T
        wide_imag = jnp.broadcast_to(bias[0, 1:2, :], (lanes, chans)).T
        bias_to[...] = jnp.where(real_lane, wide_real, wide_imag)

    prepare(w_in, b_in, mix_in, pull_in, bias_in)
    prepare(w_out, b_out, mix_out, pull_out, bias_out)
    acc_in[...] = jnp.zeros_like(acc_in)
    acc_out[...] = jnp.zeros_like(acc_out)
    for step in order[1:] + [0]:
        table_loads[step].wait()
    load_low.wait()

    mean = group_total(0, stat_copies, 0) / all_chans
    square = group_total(0, [], 1) / all_chans
    stats[0] = mean
    stats[1] = lax.rsqrt(square - mean * mean + norm_eps)

    def normal_tile(at):
        part = tok[pl.ds(pl.multiple_of(at * tile, tile), tile), :].astype(jnp.float32)
        normed, normal = [], []
        for item in range(group):
            value = (part[item * rows:(item + 1) * rows, :] - stats[0]) * stats[1]
            normed.append(value)
            normal.append(value * gain[at * group + item] + shift[at * group + item])
        return part, normed, normal

    def normalize(at, carry):
        _, _, normal = normal_tile(at)
        high, low = halves(jnp.concatenate(normal, axis=0))
        part = pl.ds(pl.multiple_of(at * tile, tile), tile)
        norm_high[part, :] = high
        norm_low[part, :] = low
        return carry

    lax.fori_loop(0, all_rows // tile, normalize, 0)

    f1 = {}
    for step in order:
        d = partner(step)
        lon(f1_send.at[d], d, norm_high, norm_low)
        f1[step] = send(f1_send.at[d], f1_recv.at[me], 0, step)
    lon(f1_recv.at[me], me, norm_high, norm_low)
    for step in order[1:]:
        d = partner(step)
        lon(f2_send.at[d], d, cot, None)
        f2[step] = send(f2_send.at[d], f2_recv.at[me], 1, step)
    lon(f2_recv.at[me], me, cot, None)

    def lat_forward(src, dst, scale):
        def body(at, carry):
            for row in range(rows):
                values = [
                    src[owner, pl.ds(at * 8 * rows + row, 8, stride=rows), :] * scale
                    for owner in range(lat_count)
                ]
                values = butterflies(values, -1.0, sign, half)
                for low in range(lat_count):
                    work[row * lat_count + low] = rotate(
                        values[low], row * low, modes_all, -1.0, sign, half
                    )
            for low in range(lat_count):
                values = [work[row * lat_count + low] for row in range(rows)]
                values = butterflies(values, -1.0, sign, half)
                for high in range(rows):
                    dst[low + lat_count * high, pl.ds(pl.multiple_of(at * 8, 8), 8), :] = values[high]
            return carry

        lax.fori_loop(0, chans // 8, body, 0)

    def lat_back(src, dst, scale):
        def body(at, carry):
            for low in range(lat_count):
                values = [
                    src[low + lat_count * high, pl.ds(pl.multiple_of(at * 8, 8), 8), :] * scale
                    for high in range(rows)
                ]
                values = butterflies(values, 1.0, sign, half)
                for row in range(rows):
                    work[row * lat_count + low] = rotate(
                        values[row], row * low, modes_all, 1.0, sign, half
                    )
            for row in range(rows):
                values = [work[row * lat_count + low] for low in range(lat_count)]
                values = butterflies(values, 1.0, sign, half)
                for owner in range(lat_count):
                    dst[owner, pl.ds(at * 8 * rows + row, 8, stride=rows), :] = values[owner]
            return carry

        lax.fori_loop(0, chans // 8, body, 0)

    def stacked(pair, turn):
        turned = [turn * flip(value, half) for value in pair]
        return jnp.concatenate(
            [jnp.concatenate(pair, axis=1), jnp.concatenate(turned, axis=1)], axis=0
        )

    def mixed_by(matrix, value):
        high, low = halves(value)
        both = dot(matrix[...], high)
        return both[:chans] + both[chans:] + dot(matrix[:chans], low)

    for step in order:
        f1[step].wait_recv()
    lat_forward(f1_recv, spec, norm)

    def filter_modes(at, carry):
        pair = [spec[2 * at], spec[2 * at + 1]]
        pre = mixed_by(mix_in, stacked(pair, sign))
        pair = []
        for item in range(2):
            value = jnp.maximum(pre[:, item * lanes:(item + 1) * lanes] + bias_in[...], 0.0)
            act[2 * at + item] = value
            pair.append(value)
        post = mixed_by(mix_out, stacked(pair, sign))
        for item in range(2):
            value = post[:, item * lanes:(item + 1) * lanes] + bias_out[...]
            kept = jnp.maximum(jnp.abs(value) - shrink_level, 0.0)
            shrunk[2 * at + item] = jnp.where(value < 0.0, -kept, kept)
        return carry

    lax.fori_loop(0, modes_all // 2, filter_modes, 0)
    lat_back(shrunk, b1_send, norm * mode_weight)
    b1 = {}
    for step in order[1:]:
        b1[step] = send(b1_send.at[partner(step)], b1_recv.at[me], 2, step)

    for step in order:
        f2[step].wait_recv()
    lat_forward(f2_recv, gspec, norm * mode_weight)

    def pull_modes(at, carry):
        pair = []
        for item in range(2):
            pair.append(jnp.where(shrunk[2 * at + item] != 0.0, gspec[2 * at + item], 0.0))
        d_post = stacked(pair, -sign).astype(jnp.bfloat16)
        both = dot(pull_out[...], d_post)
        d_act = both[:chans] + both[chans:]
        acts = [act[2 * at], act[2 * at + 1]]
        left = jnp.concatenate(acts, axis=1).astype(jnp.bfloat16)
        acc_out[...] += dot_lanes(left, d_post)
        pair = []
        for item in range(2):
            value = d_act[:, item * lanes:(item + 1) * lanes]
            pair.append(jnp.where(acts[item] > 0.0, value, 0.0))
        d_pre = stacked(pair, -sign).astype(jnp.bfloat16)
        both = dot(pull_in[...], d_pre)
        d_spec = both[:chans] + both[chans:]
        left = jnp.concatenate([spec[2 * at], spec[2 * at + 1]], axis=1).astype(jnp.bfloat16)
        acc_in[...] += dot_lanes(left, d_pre)
        for item in range(2):
            gspec[2 * at + item] = d_spec[:, item * lanes:(item + 1) * lanes]
        return carry

    lax.fori_loop(0, modes_all // 2, pull_modes, 0)
    lat_back(gspec, b2_send, norm)
    b2 = {}
    for step in order:
        b2[step] = send(b2_send.at[partner(step)], b2_recv.at[me], 3, step)
    b1[first] = send(b1_send.at[partner(first)], b1_recv.at[me], 2, first)

    level = 1.0 / math.sqrt(modes_all * lat_count * half)
    gw_rows = gw_recv.shape[1]
    pieces = [acc_in[:, :chans], acc_in[:, chans:], acc_out[:, :chans], acc_out[:, chans:]]
    for at, piece in enumerate(pieces):
        for row in range(0, chans, gw_rows):
            place = (at * chans + row) // gw_rows
            gw_send[place, :, :chans] = piece[row:row + gw_rows, :] * level
    gw = {}
    for step in order:
        gw[step] = send(gw_send.at[partner(step)], gw_recv.at[step], 4, step)

    def lon_back(acc, block, d, start):
        size = 128

        def body(at, carry):
            part = pl.ds(pl.multiple_of(at * size, size), size)
            left = block[part, :].astype(jnp.bfloat16)
            for chunk in range(0, chunks, 2):
                out = dot(left, back_tab[d, :, chunk * lanes:(chunk + 2) * lanes])
                for item in range(2):
                    value = out[:, item * lanes:(item + 1) * lanes]
                    if not start:
                        value = value + acc[chunk + item, part, :]
                    acc[chunk + item, part, :] = value
            return carry

        lax.fori_loop(0, all_rows // size, body, 0)

    load_back.wait()
    field, pulled = f1_recv, f2_recv
    lon_back(field, b1_send.at[me], me, True)
    lon_back(pulled, b2_send.at[me], me, True)
    for step in order[1:]:
        b1[step].wait_recv()
        lon_back(field, b1_recv.at[partner(step)], partner(step), False)

    total = gw_send[me]
    for step in order:
        gw[step].wait_recv()
        total = total + gw_recv[step]
    gw_out[...] = total[:, :chans]

    for step in order:
        b2[step].wait_recv()
        lon_back(pulled, b2_recv.at[partner(step)], partner(step), False)

    def gathered(acc, at):
        part = pl.ds(pl.multiple_of(at * tile, tile), tile)
        return jnp.concatenate([acc[chunk, part, :] for chunk in range(chunks)], axis=1)

    def dnorm_tile(at):
        part, normed, _ = normal_tile(at)
        grad = cot[pl.ds(pl.multiple_of(at * tile, tile), tile), :].astype(jnp.float32)
        whole = grad + gathered(pulled, at)
        dnorm = [
            whole[item * rows:(item + 1) * rows, :] * gain[at * group + item]
            for item in range(group)
        ]
        return grad, normed, dnorm

    def back_sums(at, carry):
        one, two = carry
        _, normed, dnorm = dnorm_tile(at)
        for item in range(group):
            one, two = one + dnorm[item], two + dnorm[item] * normed[item]
        return one, two

    one, two = lax.fori_loop(0, all_rows // tile, back_sums, (zero, zero))
    sum_send[1, 0], sum_send[1, 1] = one, two
    back_copies = group_exchange(1)
    stats[2] = group_total(1, back_copies, 0) / all_chans
    stats[3] = group_total(1, [], 1) / all_chans

    def finish_grad(at, carry):
        grad, normed, dnorm = dnorm_tile(at)
        out = []
        for item in range(group):
            inner = dnorm[item] - stats[2] - normed[item] * stats[3]
            out.append(grad[item * rows:(item + 1) * rows, :] + stats[1] * inner)
        part = pl.ds(pl.multiple_of(at * tile, tile), tile)
        norm_low[part, :] = jnp.concatenate(out, axis=0).astype(jnp.bfloat16)
        return carry

    lax.fori_loop(0, all_rows // tile, finish_grad, 0)
    store_grad = load(norm_low, gtok_hbm, 5)

    b1[first].wait_recv()
    lon_back(field, b1_recv.at[partner(first)], partner(first), False)

    def finish_mixed(at, carry):
        part, _, normal = normal_tile(at)
        out = gathered(field, at) + jnp.concatenate(normal, axis=0) + part
        norm_high[pl.ds(pl.multiple_of(at * tile, tile), tile), :] = out.astype(jnp.bfloat16)
        return carry

    lax.fori_loop(0, all_rows // tile, finish_mixed, 0)
    store_mixed = load(norm_high, mixed_hbm, 6)

    for step in order:
        f1[step].wait_send()
        f2[step].wait_send()
        b1[step].wait_send()
        b2[step].wait_send()
        gw[step].wait_send()
    for copy in stat_copies + back_copies:
        copy.wait_send()
    store_grad.wait()
    store_mixed.wait()


def fused(lat_count, grp_count, tokens, cotangent, gain, shift, w_in, b_in, w_out, b_out):
    chans, rows, length = tokens.shape
    modes = length // 2
    lanes = 2 * (modes // lat_count)
    lat_len = rows * lat_count
    all_rows = chans * rows
    table = lon_table(length, modes, lat_count).transpose(1, 0, 2, 3)
    table = table.reshape(lat_count, length, lanes)
    high = table.astype(ml_dtypes.bfloat16)
    low = (table - high.astype(np.float32)).astype(ml_dtypes.bfloat16)
    back = np.ascontiguousarray(high.transpose(0, 2, 1))
    gw_rows = 4 * chans // lat_count
    f32, bf16 = jnp.float32, jnp.bfloat16
    block = pltpu.VMEM((lat_count, all_rows, lanes), f32)
    modal = pltpu.VMEM((lat_len, chans, lanes), f32)
    anywhere = pl.BlockSpec(memory_space=pl.ANY)
    scalars = pl.BlockSpec(memory_space=pltpu.SMEM)
    inside = pl.BlockSpec(memory_space=pltpu.VMEM)
    mixed, gtok, gw = pl.pallas_call(
        functools.partial(band_kernel, lat_count, grp_count),
        out_shape=(
            jax.ShapeDtypeStruct((all_rows, length), bf16),
            jax.ShapeDtypeStruct((all_rows, length), bf16),
            jax.ShapeDtypeStruct((gw_rows, chans), f32),
        ),
        in_specs=[anywhere] * 5 + [scalars] * 2 + [inside] * 4,
        out_specs=(anywhere, anywhere, inside),
        scratch_shapes=[
            pltpu.VMEM((all_rows, length), bf16),
            pltpu.VMEM((all_rows, length), bf16),
            pltpu.VMEM((lat_count, length, lanes), bf16),
            pltpu.VMEM((lat_count, length, lanes), bf16),
            pltpu.VMEM((lat_count, lanes, length), bf16),
            pltpu.VMEM((all_rows, length), bf16),
            pltpu.VMEM((all_rows, length), bf16),
            *[block] * 8,
            *[modal] * 4,
            pltpu.VMEM((lat_len, 8, lanes), f32),
            pltpu.VMEM((4, rows, length), f32),
            pltpu.VMEM((2, 2, rows, length), f32),
            pltpu.VMEM((2, grp_count, 2, rows, length), f32),
            *[pltpu.VMEM((2 * chans, 2 * chans), bf16)] * 4,
            *[pltpu.VMEM((chans, lanes), f32)] * 2,
            *[pltpu.VMEM((chans, 2 * chans), f32)] * 2,
            pltpu.VMEM((lat_count, gw_rows, lanes), f32),
            pltpu.VMEM((lat_count, gw_rows, lanes), f32),
            pltpu.SemaphoreType.DMA((7 * lat_count,)),
            pltpu.SemaphoreType.DMA((7 * lat_count,)),
            pltpu.SemaphoreType.DMA((8 + lat_count,)),
        ],
        compiler_params=pltpu.CompilerParams(
            collective_id=0, has_side_effects=True, vmem_limit_bytes=60 << 20
        ),
    )(
        tokens.reshape(all_rows, length), cotangent.reshape(all_rows, length),
        jnp.asarray(high), jnp.asarray(low), jnp.asarray(back),
        gain, shift, w_in, b_in, w_out, b_out,
    )
    return (
        mixed.reshape(chans, rows, length), gtok.reshape(chans, rows, length), gw.reshape(1, -1)
    )


def fits(lat_count, grp_count, tokens):
    chans, rows, length = tokens.shape
    lanes = length // lat_count
    gw_rows = 4 * chans // lat_count
    return (
        lanes == 128 and lat_count & (lat_count - 1) == 0 and rows == 8
        and grp_count <= lat_count and chans % gw_rows == 0 and gw_rows % 8 == 0
        and (chans * rows) % 256 == 0 and chans % 16 == 0 and chans <= lanes
    )


def per_part(*args):
    lat_count, grp_count = lax.axis_size("lat"), lax.axis_size("grp")
    if fits(lat_count, grp_count, args[0]):
        return fused(lat_count, grp_count, *args)
    return per_device(*args)


def solution(mesh):
    in_specs = (
        P("grp", "lat", None),
        P("grp", "lat", None),
        P("grp"),
        P("grp"),
        P("grp", None, None, None),
        P("grp", None, None),
        P("grp", None, None, None),
        P("grp", None, None),
    )
    out_specs = (P("grp", "lat", None), P("grp", "lat", None), P("grp", "lat"))
    return jax.shard_map(
        per_part, mesh=mesh, in_specs=in_specs, out_specs=out_specs, check_vma=False
    )
```

```python
import functools
import math

import numpy as np
import ml_dtypes
import jax
import jax.numpy as jnp
from jax import lax
from jax.experimental import pallas as pl
from jax.experimental.pallas import tpu as pltpu
from jax.sharding import PartitionSpec as P

shrink_level = 0.01
norm_eps = 1e-05


precise = lax.Precision.HIGH
exact = lax.Precision.HIGHEST


def contract(form, left, right, level=precise):
    return jnp.einsum(form, left, right, precision=level, preferred_element_type=jnp.float32)


def angles(left_count, right_count, length):
    phase = np.arange(left_count)[:, None] * np.arange(right_count)[None, :] % length
    theta = phase * (2.0 * math.pi / length)
    return np.cos(theta), np.sin(theta)


def lon_table(length, modes, owners):
    cos_tab, sin_tab = angles(length, modes, length)
    both = np.stack([cos_tab, -sin_tab]) / math.sqrt(length)
    both = both.reshape(2, length, owners, modes // owners)
    return both.transpose(1, 2, 0, 3).astype(np.float32)


def lat_table(length):
    cos_tab, sin_tab = angles(length, length, length)
    table = np.stack([np.stack([cos_tab, -sin_tab]), np.stack([sin_tab, cos_tab])])
    return (table / math.sqrt(length)).transpose(2, 0, 3, 1).astype(np.float32)


def group_sum(value, name):
    count = lax.axis_size(name)
    total = value
    for step in range(1, count):
        pairs = [(at, (at + step) % count) for at in range(count)]
        total = total + lax.ppermute(value, name, pairs)
    return total


def scatter_sum(pieces, name):
    count = lax.axis_size(name)
    own = lax.axis_index(name)
    total = lax.dynamic_slice_in_dim(pieces, own, 1, axis=0)
    for step in range(1, count):
        pairs = [(at, (at + step) % count) for at in range(count)]
        piece = lax.dynamic_slice_in_dim(pieces, (own + step) % count, 1, axis=0)
        total = total + lax.ppermute(piece, name, pairs)
    return total


def swap(value):
    return lax.all_to_all(value, "lat", split_axis=0, concat_axis=0, tiled=True)


def mix_matrix(weight):
    real_part, imag_part = weight[0], weight[1]
    top = jnp.stack([real_part, imag_part], axis=1)
    low = jnp.stack([-imag_part, real_part], axis=1)
    return jnp.stack([top, low])


def shrink(value):
    return jnp.sign(value) * jnp.maximum(jnp.abs(value) - shrink_level, 0.0)


def matrix_grad(full):
    real_part = full[0, :, 0] + full[1, :, 1]
    imag_part = full[0, :, 1] - full[1, :, 0]
    return real_part, imag_part


def per_device(tokens, cotangent, gain, shift, w_in, b_in, w_out, b_out):
    chans, rows, length = tokens.shape
    lat_count = lax.axis_size("lat")
    all_chans = chans * lax.axis_size("grp")
    modes = length // 2
    own = modes // lat_count
    lat_len = rows * lat_count
    table = lon_table(length, modes, lat_count).reshape(length, 2 * modes)
    table = jnp.asarray(table)
    lat_tab = jnp.asarray(lat_table(lat_len)).reshape(lat_count, rows, 2, lat_len, 2)
    tok_val = tokens.astype(jnp.float32)
    grad_val = cotangent.astype(jnp.float32)

    def lon_parts(field, level):
        out = contract("crn,ndq->dcrq", field, table.reshape(length, lat_count, 2 * own), level)
        return out.reshape(lat_count, chans * rows, 2 * own)

    def lat_in(parts, level):
        parts = parts.reshape(lat_count, chans, rows, 2, own)
        return contract("scrim,srikj->kmjc", parts, lat_tab, level)

    def lat_out(value):
        out = contract("kmjc,srikj->scrim", value, lat_tab)
        return out.reshape(lat_count, chans * rows, 2 * own)

    def lon_back(parts):
        parts = parts.reshape(lat_count, chans, rows, 2 * own)
        return contract("dcrq,ndq->crn", parts, table.reshape(length, lat_count, 2 * own))

    sums = jnp.stack([jnp.sum(tok_val, axis=0), jnp.sum(tok_val * tok_val, axis=0)])
    sums = group_sum(sums, "grp")
    token_mean = sums[0] / all_chans
    inv_std = lax.rsqrt(sums[1] / all_chans - token_mean * token_mean + norm_eps)
    normed = (tok_val - token_mean) * inv_std
    normal_out = normed * gain[:, None, None] + shift[:, None, None]
    send_field, grad_val = lax.optimization_barrier((lon_parts(normal_out, exact), grad_val))
    recv_field = swap(send_field)
    recv_grad = swap(lon_parts(grad_val, precise))

    mat_in, mat_out = mix_matrix(w_in[0]), mix_matrix(w_out[0])
    at_mode = lax.axis_index("lat") * own + jnp.arange(own)
    mode_weight = jnp.where(at_mode == 0, 1.0, 2.0).astype(jnp.float32)[None, :, None, None]
    spec = lat_in(recv_field, exact)
    pre = contract("kmic,icjo->kmjo", spec, mat_in, exact) + b_in[0]
    act = jax.nn.relu(pre)
    post = contract("kmic,icjo->kmjo", act, mat_out, exact) + b_out[0]
    back_field = lat_out(shrink(post) * mode_weight)
    back_field, spec, pre, act, post, recv_grad = lax.optimization_barrier(
        (back_field, spec, pre, act, post, recv_grad)
    )
    rows_field = swap(back_field)

    grad = lat_in(recv_grad, precise) * mode_weight
    d_post = jnp.where(jnp.abs(post) > shrink_level, grad, 0.0)
    d_act = contract("kmjo,icjo->kmic", d_post, mat_out)
    d_pre = jnp.where(pre > 0.0, d_act, 0.0)
    d_spec = contract("kmjo,icjo->kmic", d_pre, mat_in)
    back_grad, spec, act, d_post, d_pre = lax.optimization_barrier(
        (lat_out(d_spec), spec, act, d_post, d_pre)
    )
    rows_grad = swap(back_grad)
    full_out = contract("kmic,kmjo->icjo", act, d_post)
    full_in = contract("kmic,kmjo->icjo", spec, d_pre)
    grads = jnp.stack([*matrix_grad(full_in), *matrix_grad(full_out)])
    grads = grads.reshape(lat_count, -1) * (1.0 / math.sqrt(lat_len * modes))
    grad_weights = scatter_sum(grads, "lat")

    mixed = (lon_back(rows_field) + normal_out + tok_val).astype(jnp.bfloat16)
    dnorm = (grad_val + lon_back(rows_grad)) * gain[:, None, None]
    back = group_sum(jnp.stack([jnp.sum(dnorm, axis=0), jnp.sum(dnorm * normed, axis=0)]), "grp")
    grad_tokens = grad_val + inv_std * (
        dnorm - back[0] / all_chans - normed * (back[1] / all_chans)
    )
    return (mixed, grad_tokens.astype(jnp.bfloat16), grad_weights)


MESH = pl.DeviceIdType.MESH


def flip(value, half):
    return pltpu.roll(value, half, value.ndim - 1)


def rotate(value, step, count, sense, sign, half):
    step = step % count
    if step == 0:
        return value
    if 2 * step == count:
        return -value
    angle = sense * 2.0 * math.pi * step / count
    turned = sign * flip(value, half)
    if 4 * step == count or 4 * step == 3 * count:
        return turned if math.sin(angle) > 0 else -turned
    return value * math.cos(angle) + turned * math.sin(angle)


def butterflies(values, sense, sign, half):
    count = len(values)
    if count == 1:
        return values
    even = butterflies(values[0::2], sense, sign, half)
    odd = butterflies(values[1::2], sense, sign, half)
    low, high = [], []
    for at in range(count // 2):
        turned = rotate(odd[at], at, count, sense, sign, half)
        low.append(even[at] + turned)
        high.append(even[at] - turned)
    return low + high


def dot(left, right):
    return lax.dot_general(
        left, right, (((1,), (0,)), ((), ())), preferred_element_type=jnp.float32
    )


def dot_lanes(left, right):
    return lax.dot_general(
        left, right, (((1,), (1,)), ((), ())), preferred_element_type=jnp.float32
    )


def halves(value):
    high = value.astype(jnp.bfloat16)
    return high, (value - high.astype(jnp.float32)).astype(jnp.bfloat16)


def band_kernel(
    lat_count, grp_count,
    tok_hbm, cot_hbm, high_hbm, low_hbm, back_hbm, gain, shift, w_in, b_in, w_out, b_out,
    mixed_hbm, gtok_hbm, gw_out,
    tok, cot, high_tab, low_tab, back_tab, norm_high, norm_low,
    f1_send, f1_recv, f2_send, f2_recv, b1_send, b1_recv, b2_send, b2_recv,
    spec, act, shrunk, gspec, work, stats, sum_send, sum_recv,
    mix_in, mix_out, pull_in, pull_out, bias_in, bias_out, acc_in, acc_out,
    gw_send, gw_recv, send_sem, recv_sem, load_sem,
):
    me, grp = lax.axis_index("lat"), lax.axis_index("grp")
    modes_all, chans, lanes = spec.shape
    half = lanes // 2
    all_rows, length = tok.shape
    rows = all_rows // chans
    chunks = length // lanes
    all_chans = chans * grp_count
    group = 16 // rows if rows < 16 else 1
    tile = group * rows
    piece_rows = 128

    def partner(step):
        other, bit = me, 1
        while bit < lat_count:
            if step & bit:
                other = other + bit * (1 - 2 * lax.rem(lax.div(me, bit), 2))
            bit *= 2
        return other

    def send(src, dst, kind, step):
        copy = pltpu.make_async_remote_copy(
            src_ref=src, dst_ref=dst,
            send_sem=send_sem.at[kind * lat_count + step],
            recv_sem=recv_sem.at[kind * lat_count + step],
            device_id=(partner(step), grp), device_id_type=MESH,
        )
        copy.start()
        return copy

    def load(src, dst, at):
        copy = pltpu.make_async_copy(src, dst, load_sem.at[at])
        copy.start()
        return copy

    far, near = list(range(lat_count // 2, lat_count)), list(range(1, lat_count // 2))
    first, held = far[0], far[-1]
    f1_order = [*near[-1:], *far[1:], *near[:-1], first]
    f2_order = f1_order[:-1]
    b1_order = [*near[-1:], *far[:-1], *near[:-1]]
    b2_order = [*near[-1:], *far, *near[:-1]]

    load_cot = load(cot_hbm, cot, 0)
    load_first = load(high_hbm.at[partner(first)], high_tab.at[partner(first)], 1)
    load_tok = load(tok_hbm, tok, 2)
    table_loads = {}
    for step in f2_order + [0]:
        d = partner(step)
        table_loads[step] = load(high_hbm.at[d], high_tab.at[d], 8 + step)
    load_low = load(low_hbm, low_tab, 3)
    load_back = load(back_hbm, back_tab, 4)

    barrier = pltpu.get_barrier_semaphore()
    for step in range(1, lat_count):
        pl.semaphore_signal(barrier, inc=1, device_id=(partner(step), grp), device_id_type=MESH)
    for step in range(1, grp_count):
        pl.semaphore_signal(
            barrier, inc=1, device_id=(me, lax.rem(grp + step, grp_count)), device_id_type=MESH
        )

    lane = lax.broadcasted_iota(jnp.int32, (1, lanes), 1)
    real_lane = lane < half
    sign = jnp.where(real_lane, -1.0, 1.0).astype(jnp.float32)
    at_mode = jnp.where(real_lane, lane, lane - half) + me * half
    mode_weight = jnp.where(at_mode == 0, 1.0, 2.0).astype(jnp.float32)
    norm = 1.0 / math.sqrt(modes_all)

    def lon(dst, d, left_high, left_low, full=True):
        size = min(256, all_rows)

        def body(at, carry):
            part = pl.ds(pl.multiple_of(at * size, size), size)
            out = dot(left_high[part, :], high_tab[d])
            if left_low is not None:
                out = out + dot(left_low[part, :], high_tab[d])
            if full:
                out = out + dot(left_high[part, :], low_tab[d])
            dst[part, :] = out
            return carry

        lax.fori_loop(0, all_rows // size, body, 0)

    def group_exchange(use):
        copies = []
        for step in range(1, grp_count):
            copy = pltpu.make_async_remote_copy(
                src_ref=sum_send.at[use], dst_ref=sum_recv.at[use, step],
                send_sem=send_sem.at[(5 + use) * lat_count + step],
                recv_sem=recv_sem.at[(5 + use) * lat_count + step],
                device_id=(me, lax.rem(grp + step, grp_count)), device_id_type=MESH,
            )
            copy.start()
            copies.append(copy)
        return copies

    def group_total(use, copies, at):
        for copy in copies:
            copy.wait_recv()
        total = sum_send[use, at]
        for step in range(1, grp_count):
            total = total + sum_recv[use, step, at]
        return total

    load_cot.wait()
    load_first.wait()
    lon(f2_send.at[partner(first)], partner(first), cot, None, False)
    pl.semaphore_wait(barrier, lat_count - 1 + grp_count - 1)
    f2 = {first: send(f2_send.at[partner(first)], f2_recv.at[me], 1, first)}

    load_tok.wait()

    def sums(at, carry):
        one, two = carry
        part = tok[pl.ds(pl.multiple_of(at * tile, tile), tile), :].astype(jnp.float32)
        for item in range(group):
            value = part[item * rows:(item + 1) * rows, :]
            one, two = one + value, two + value * value
        return one, two

    zero = jnp.zeros((rows, length), jnp.float32)
    one, two = lax.fori_loop(0, all_rows // tile, sums, (zero, zero))
    sum_send[0, 0], sum_send[0, 1] = one, two
    stat_copies = group_exchange(0)

    def prepare(weight, bias, mix, pull, bias_to):
        real_part, imag_part = weight[0, 0], weight[0, 1]
        forward = jnp.concatenate([real_part, imag_part], axis=0).T
        high, low = halves(forward)
        mix[:chans], mix[chans:] = high, low
        backward = jnp.concatenate([real_part.T, imag_part.T], axis=0).T
        high, low = halves(backward)
        pull[:chans], pull[chans:] = high, low
        wide_real = jnp.broadcast_to(bias[0, 0:1, :], (lanes, chans)).T
        wide_imag = jnp.broadcast_to(bias[0, 1:2, :], (lanes, chans)).T
        bias_to[...] = jnp.where(real_lane, wide_real, wide_imag)

    prepare(w_in, b_in, mix_in, pull_in, bias_in)
    prepare(w_out, b_out, mix_out, pull_out, bias_out)
    acc_in[...] = jnp.zeros_like(acc_in)
    acc_out[...] = jnp.zeros_like(acc_out)
    for step in f2_order + [0]:
        table_loads[step].wait()
    load_low.wait()

    mean = group_total(0, stat_copies, 0) / all_chans
    square = group_total(0, [], 1) / all_chans
    stats[0] = mean
    stats[1] = lax.rsqrt(square - mean * mean + norm_eps)

    def normal_tile(at):
        part = tok[pl.ds(pl.multiple_of(at * tile, tile), tile), :].astype(jnp.float32)
        normed, normal = [], []
        for item in range(group):
            value = (part[item * rows:(item + 1) * rows, :] - stats[0]) * stats[1]
            normed.append(value)
            normal.append(value * gain[at * group + item] + shift[at * group + item])
        return part, normed, normal

    def normalize(at, carry):
        _, _, normal = normal_tile(at)
        high, low = halves(jnp.concatenate(normal, axis=0))
        part = pl.ds(pl.multiple_of(at * tile, tile), tile)
        norm_high[part, :] = high
        norm_low[part, :] = low
        return carry

    lax.fori_loop(0, all_rows // tile, normalize, 0)

    f1 = {}
    for step in f1_order:
        d = partner(step)
        lon(f1_send.at[d], d, norm_high, norm_low)
        f1[step] = send(f1_send.at[d], f1_recv.at[me], 0, step)
    lon(f1_recv.at[me], me, norm_high, norm_low)
    for step in f2_order:
        d = partner(step)
        lon(f2_send.at[d], d, cot, None)
        f2[step] = send(f2_send.at[d], f2_recv.at[me], 1, step)
    lon(f2_recv.at[me], me, cot, None)

    def lat_forward(src, dst, scale):
        def body(at, carry):
            for row in range(rows):
                values = [
                    src[owner, pl.ds(at * 8 * rows + row, 8, stride=rows), :] * scale
                    for owner in range(lat_count)
                ]
                values = butterflies(values, -1.0, sign, half)
                for low in range(lat_count):
                    work[row * lat_count + low] = rotate(
                        values[low], row * low, modes_all, -1.0, sign, half
                    )
            for low in range(lat_count):
                values = [work[row * lat_count + low] for row in range(rows)]
                values = butterflies(values, -1.0, sign, half)
                for high in range(rows):
                    dst[low + lat_count * high, pl.ds(pl.multiple_of(at * 8, 8), 8), :] = values[high]
            return carry

        lax.fori_loop(0, chans // 8, body, 0)

    def lat_back(src, dst, scale):
        def body(at, carry):
            for low in range(lat_count):
                values = [
                    src[low + lat_count * high, pl.ds(pl.multiple_of(at * 8, 8), 8), :] * scale
                    for high in range(rows)
                ]
                values = butterflies(values, 1.0, sign, half)
                for row in range(rows):
                    work[row * lat_count + low] = rotate(
                        values[row], row * low, modes_all, 1.0, sign, half
                    )
            for row in range(rows):
                values = [work[row * lat_count + low] for low in range(lat_count)]
                values = butterflies(values, 1.0, sign, half)
                for owner in range(lat_count):
                    dst[owner, pl.ds(at * 8 * rows + row, 8, stride=rows), :] = values[owner]
            return carry

        lax.fori_loop(0, chans // 8, body, 0)

    def stacked(pair, turn):
        turned = [turn * flip(value, half) for value in pair]
        return jnp.concatenate(
            [jnp.concatenate(pair, axis=1), jnp.concatenate(turned, axis=1)], axis=0
        )

    def mixed_by(matrix, value):
        high, low = halves(value)
        both = dot(matrix[...], high)
        return both[:chans] + both[chans:] + dot(matrix[:chans], low)

    for step in f1_order:
        f1[step].wait_recv()
    lat_forward(f1_recv, spec, norm)

    def filter_modes(at, carry):
        pair = [spec[2 * at], spec[2 * at + 1]]
        pre = mixed_by(mix_in, stacked(pair, sign))
        pair = []
        for item in range(2):
            value = jnp.maximum(pre[:, item * lanes:(item + 1) * lanes] + bias_in[...], 0.0)
            act[2 * at + item] = value
            pair.append(value)
        post = mixed_by(mix_out, stacked(pair, sign))
        for item in range(2):
            value = post[:, item * lanes:(item + 1) * lanes] + bias_out[...]
            kept = jnp.maximum(jnp.abs(value) - shrink_level, 0.0)
            shrunk[2 * at + item] = jnp.where(value < 0.0, -kept, kept)
        return carry

    lax.fori_loop(0, modes_all // 2, filter_modes, 0)
    lat_back(shrunk, b1_send, norm * mode_weight)
    b1 = {}
    for step in b1_order:
        b1[step] = send(b1_send.at[partner(step)], b1_recv.at[me], 2, step)

    for step in [first, *f2_order]:
        f2[step].wait_recv()
    lat_forward(f2_recv, gspec, norm * mode_weight)

    def pull_modes(at, carry):
        pair = []
        for item in range(2):
            pair.append(jnp.where(shrunk[2 * at + item] != 0.0, gspec[2 * at + item], 0.0))
        d_post = stacked(pair, -sign).astype(jnp.bfloat16)
        both = dot(pull_out[...], d_post)
        d_act = both[:chans] + both[chans:]
        acts = [act[2 * at], act[2 * at + 1]]
        high, low = halves(jnp.concatenate(acts, axis=1))
        acc_out[...] += dot_lanes(high, d_post) + dot_lanes(low, d_post)
        pair = []
        for item in range(2):
            value = d_act[:, item * lanes:(item + 1) * lanes]
            pair.append(jnp.where(acts[item] > 0.0, value, 0.0))
        d_pre = stacked(pair, -sign).astype(jnp.bfloat16)
        both = dot(pull_in[...], d_pre)
        d_spec = both[:chans] + both[chans:]
        high, low = halves(jnp.concatenate([spec[2 * at], spec[2 * at + 1]], axis=1))
        acc_in[...] += dot_lanes(high, d_pre) + dot_lanes(low, d_pre)
        for item in range(2):
            gspec[2 * at + item] = d_spec[:, item * lanes:(item + 1) * lanes]
        return carry

    lax.fori_loop(0, modes_all // 2, pull_modes, 0)
    level = 1.0 / math.sqrt(modes_all * lat_count * half)
    gw_rows = gw_recv.shape[1]
    pieces = [acc_in[:, :chans], acc_in[:, chans:], acc_out[:, :chans], acc_out[:, chans:]]
    for at, piece in enumerate(pieces):
        for row in range(0, chans, gw_rows):
            place = (at * chans + row) // gw_rows
            gw_send[place, :, :chans] = piece[row:row + gw_rows, :] * level
    gw = {}
    for step in b2_order:
        gw[step] = send(gw_send.at[partner(step)], gw_recv.at[step], 4, step)

    lat_back(gspec, b2_send, norm)
    b2 = {}
    for step in b2_order:
        b2[step] = send(b2_send.at[partner(step)], b2_recv.at[me], 3, step)
    last = []
    for at in range(all_rows // piece_rows):
        part = pl.ds(at * piece_rows, piece_rows)
        copy = pltpu.make_async_remote_copy(
            src_ref=b1_send.at[partner(held), part], dst_ref=b1_recv.at[me, part],
            send_sem=send_sem.at[7 * lat_count + at], recv_sem=recv_sem.at[7 * lat_count + at],
            device_id=(partner(held), grp), device_id_type=MESH,
        )
        copy.start()
        last.append(copy)

    def lon_back_part(acc, block, d, part, start):
        left = block[part, :].astype(jnp.bfloat16)
        for chunk in range(0, chunks, 2):
            out = dot(left, back_tab[d, :, chunk * lanes:(chunk + 2) * lanes])
            for item in range(2):
                value = out[:, item * lanes:(item + 1) * lanes]
                if not start:
                    value = value + acc[chunk + item, part, :]
                acc[chunk + item, part, :] = value

    def lon_back(acc, block, d, start):
        def body(at, carry):
            part = pl.ds(pl.multiple_of(at * piece_rows, piece_rows), piece_rows)
            lon_back_part(acc, block, d, part, start)
            return carry

        lax.fori_loop(0, all_rows // piece_rows, body, 0)

    load_back.wait()
    field, pulled = f1_recv, f2_recv
    lon_back(field, b1_send.at[me], me, True)
    lon_back(pulled, b2_send.at[me], me, True)
    for step in b1_order:
        b1[step].wait_recv()
        lon_back(field, b1_recv.at[partner(step)], partner(step), False)

    for step in b2_order:
        b2[step].wait_recv()
        lon_back(pulled, b2_recv.at[partner(step)], partner(step), False)

    def gathered(acc, at):
        part = pl.ds(pl.multiple_of(at * tile, tile), tile)
        return jnp.concatenate([acc[chunk, part, :] for chunk in range(chunks)], axis=1)

    def dnorm_tile(at):
        part, normed, _ = normal_tile(at)
        grad = cot[pl.ds(pl.multiple_of(at * tile, tile), tile), :].astype(jnp.float32)
        whole = grad + gathered(pulled, at)
        dnorm = [
            whole[item * rows:(item + 1) * rows, :] * gain[at * group + item]
            for item in range(group)
        ]
        return grad, normed, dnorm

    def back_sums(at, carry):
        one, two = carry
        _, normed, dnorm = dnorm_tile(at)
        for item in range(group):
            one, two = one + dnorm[item], two + dnorm[item] * normed[item]
        return one, two

    one, two = lax.fori_loop(0, all_rows // tile, back_sums, (zero, zero))
    sum_send[1, 0], sum_send[1, 1] = one, two
    back_copies = group_exchange(1)
    stats[2] = group_total(1, back_copies, 0) / all_chans
    stats[3] = group_total(1, [], 1) / all_chans

    def finish_grad(at, carry):
        grad, normed, dnorm = dnorm_tile(at)
        out = []
        for item in range(group):
            inner = dnorm[item] - stats[2] - normed[item] * stats[3]
            out.append(grad[item * rows:(item + 1) * rows, :] + stats[1] * inner)
        part = pl.ds(pl.multiple_of(at * tile, tile), tile)
        norm_low[part, :] = jnp.concatenate(out, axis=0).astype(jnp.bfloat16)
        return carry

    lax.fori_loop(0, all_rows // tile, finish_grad, 0)
    store_grad = load(norm_low, gtok_hbm, 5)

    total = gw_send[me]
    for step in b2_order:
        gw[step].wait_recv()
        total = total + gw_recv[step]
    gw_out[...] = total[:, :chans]

    def finish_mixed(at, carry):
        part, _, normal = normal_tile(at)
        out = gathered(field, at) + jnp.concatenate(normal, axis=0) + part
        norm_high[pl.ds(pl.multiple_of(at * tile, tile), tile), :] = out.astype(jnp.bfloat16)
        return carry

    stores = []
    for at, copy in enumerate(last):
        copy.wait_recv()
        part = pl.ds(at * piece_rows, piece_rows)
        lon_back_part(field, b1_recv.at[partner(held)], partner(held), part, False)
        tiles = piece_rows // tile
        lax.fori_loop(at * tiles, (at + 1) * tiles, finish_mixed, 0)
        stores.append(load(norm_high.at[part], mixed_hbm.at[part], 8 + lat_count + at))

    for step in b2_order:
        f1[step].wait_send()
        f2[step].wait_send()
        if step != held:
            b1[step].wait_send()
        b2[step].wait_send()
        gw[step].wait_send()
    for copy in stat_copies + back_copies + last:
        copy.wait_send()
    store_grad.wait()
    for store in stores:
        store.wait()


def fused(lat_count, grp_count, tokens, cotangent, gain, shift, w_in, b_in, w_out, b_out):
    chans, rows, length = tokens.shape
    modes = length // 2
    lanes = 2 * (modes // lat_count)
    lat_len = rows * lat_count
    all_rows = chans * rows
    table = lon_table(length, modes, lat_count).transpose(1, 0, 2, 3)
    table = table.reshape(lat_count, length, lanes)
    high = table.astype(ml_dtypes.bfloat16)
    low = (table - high.astype(np.float32)).astype(ml_dtypes.bfloat16)
    back = np.ascontiguousarray(high.transpose(0, 2, 1))
    gw_rows = 4 * chans // lat_count
    f32, bf16 = jnp.float32, jnp.bfloat16
    block = pltpu.VMEM((lat_count, all_rows, lanes), f32)
    modal = pltpu.VMEM((lat_len, chans, lanes), f32)
    anywhere = pl.BlockSpec(memory_space=pl.ANY)
    scalars = pl.BlockSpec(memory_space=pltpu.SMEM)
    inside = pl.BlockSpec(memory_space=pltpu.VMEM)
    mixed, gtok, gw = pl.pallas_call(
        functools.partial(band_kernel, lat_count, grp_count),
        out_shape=(
            jax.ShapeDtypeStruct((all_rows, length), bf16),
            jax.ShapeDtypeStruct((all_rows, length), bf16),
            jax.ShapeDtypeStruct((gw_rows, chans), f32),
        ),
        in_specs=[anywhere] * 5 + [scalars] * 2 + [inside] * 4,
        out_specs=(anywhere, anywhere, inside),
        scratch_shapes=[
            pltpu.VMEM((all_rows, length), bf16),
            pltpu.VMEM((all_rows, length), bf16),
            pltpu.VMEM((lat_count, length, lanes), bf16),
            pltpu.VMEM((lat_count, length, lanes), bf16),
            pltpu.VMEM((lat_count, lanes, length), bf16),
            pltpu.VMEM((all_rows, length), bf16),
            pltpu.VMEM((all_rows, length), bf16),
            *[block] * 8,
            *[modal] * 4,
            pltpu.VMEM((lat_len, 8, lanes), f32),
            pltpu.VMEM((4, rows, length), f32),
            pltpu.VMEM((2, 2, rows, length), f32),
            pltpu.VMEM((2, grp_count, 2, rows, length), f32),
            *[pltpu.VMEM((2 * chans, 2 * chans), bf16)] * 4,
            *[pltpu.VMEM((chans, lanes), f32)] * 2,
            *[pltpu.VMEM((chans, 2 * chans), f32)] * 2,
            pltpu.VMEM((lat_count, gw_rows, lanes), f32),
            pltpu.VMEM((lat_count, gw_rows, lanes), f32),
            pltpu.SemaphoreType.DMA((7 * lat_count + all_rows // 128,)),
            pltpu.SemaphoreType.DMA((7 * lat_count + all_rows // 128,)),
            pltpu.SemaphoreType.DMA((8 + lat_count + all_rows // 128,)),
        ],
        compiler_params=pltpu.CompilerParams(
            collective_id=0, has_side_effects=True, vmem_limit_bytes=60 << 20
        ),
    )(
        tokens.reshape(all_rows, length), cotangent.reshape(all_rows, length),
        jnp.asarray(high), jnp.asarray(low), jnp.asarray(back),
        gain, shift, w_in, b_in, w_out, b_out,
    )
    return (
        mixed.reshape(chans, rows, length), gtok.reshape(chans, rows, length), gw.reshape(1, -1)
    )


def fits(lat_count, grp_count, tokens):
    chans, rows, length = tokens.shape
    lanes = length // lat_count
    gw_rows = 4 * chans // lat_count
    return (
        lanes == 128 and lat_count & (lat_count - 1) == 0 and rows == 8
        and grp_count <= lat_count and chans % gw_rows == 0 and gw_rows % 8 == 0
        and (chans * rows) % 256 == 0 and chans % 16 == 0 and chans <= lanes
    )


def per_part(*args):
    lat_count, grp_count = lax.axis_size("lat"), lax.axis_size("grp")
    if fits(lat_count, grp_count, args[0]):
        return fused(lat_count, grp_count, *args)
    return per_device(*args)


def solution(mesh):
    in_specs = (
        P("grp", "lat", None),
        P("grp", "lat", None),
        P("grp"),
        P("grp"),
        P("grp", None, None, None),
        P("grp", None, None),
        P("grp", None, None, None),
        P("grp", None, None),
    )
    out_specs = (P("grp", "lat", None), P("grp", "lat", None), P("grp", "lat"))
    return jax.shard_map(
        per_part, mesh=mesh, in_specs=in_specs, out_specs=out_specs, check_vma=False
    )
```

```python
import functools
import math

import numpy as np
import ml_dtypes
import jax
import jax.numpy as jnp
from jax import lax
from jax.experimental import pallas as pl
from jax.experimental.pallas import tpu as pltpu
from jax.sharding import PartitionSpec as P

shrink_level = 0.01
norm_eps = 1e-05


precise = lax.Precision.HIGH
exact = lax.Precision.HIGHEST


def contract(form, left, right, level=precise):
    return jnp.einsum(form, left, right, precision=level, preferred_element_type=jnp.float32)


def angles(left_count, right_count, length):
    phase = np.arange(left_count)[:, None] * np.arange(right_count)[None, :] % length
    theta = phase * (2.0 * math.pi / length)
    return np.cos(theta), np.sin(theta)


def lon_table(length, modes, owners):
    cos_tab, sin_tab = angles(length, modes, length)
    both = np.stack([cos_tab, -sin_tab]) / math.sqrt(length)
    both = both.reshape(2, length, owners, modes // owners)
    return both.transpose(1, 2, 0, 3).astype(np.float32)


def lat_table(length):
    cos_tab, sin_tab = angles(length, length, length)
    table = np.stack([np.stack([cos_tab, -sin_tab]), np.stack([sin_tab, cos_tab])])
    return (table / math.sqrt(length)).transpose(2, 0, 3, 1).astype(np.float32)


def group_sum(value, name):
    count = lax.axis_size(name)
    total = value
    for step in range(1, count):
        pairs = [(at, (at + step) % count) for at in range(count)]
        total = total + lax.ppermute(value, name, pairs)
    return total


def scatter_sum(pieces, name):
    count = lax.axis_size(name)
    own = lax.axis_index(name)
    total = lax.dynamic_slice_in_dim(pieces, own, 1, axis=0)
    for step in range(1, count):
        pairs = [(at, (at + step) % count) for at in range(count)]
        piece = lax.dynamic_slice_in_dim(pieces, (own + step) % count, 1, axis=0)
        total = total + lax.ppermute(piece, name, pairs)
    return total


def swap(value):
    return lax.all_to_all(value, "lat", split_axis=0, concat_axis=0, tiled=True)


def mix_matrix(weight):
    real_part, imag_part = weight[0], weight[1]
    top = jnp.stack([real_part, imag_part], axis=1)
    low = jnp.stack([-imag_part, real_part], axis=1)
    return jnp.stack([top, low])


def shrink(value):
    return jnp.sign(value) * jnp.maximum(jnp.abs(value) - shrink_level, 0.0)


def matrix_grad(full):
    real_part = full[0, :, 0] + full[1, :, 1]
    imag_part = full[0, :, 1] - full[1, :, 0]
    return real_part, imag_part


def per_device(tokens, cotangent, gain, shift, w_in, b_in, w_out, b_out):
    chans, rows, length = tokens.shape
    lat_count = lax.axis_size("lat")
    all_chans = chans * lax.axis_size("grp")
    modes = length // 2
    own = modes // lat_count
    lat_len = rows * lat_count
    table = lon_table(length, modes, lat_count).reshape(length, 2 * modes)
    table = jnp.asarray(table)
    lat_tab = jnp.asarray(lat_table(lat_len)).reshape(lat_count, rows, 2, lat_len, 2)
    tok_val = tokens.astype(jnp.float32)
    grad_val = cotangent.astype(jnp.float32)

    def lon_parts(field, level):
        out = contract("crn,ndq->dcrq", field, table.reshape(length, lat_count, 2 * own), level)
        return out.reshape(lat_count, chans * rows, 2 * own)

    def lat_in(parts, level):
        parts = parts.reshape(lat_count, chans, rows, 2, own)
        return contract("scrim,srikj->kmjc", parts, lat_tab, level)

    def lat_out(value):
        out = contract("kmjc,srikj->scrim", value, lat_tab)
        return out.reshape(lat_count, chans * rows, 2 * own)

    def lon_back(parts):
        parts = parts.reshape(lat_count, chans, rows, 2 * own)
        return contract("dcrq,ndq->crn", parts, table.reshape(length, lat_count, 2 * own))

    sums = jnp.stack([jnp.sum(tok_val, axis=0), jnp.sum(tok_val * tok_val, axis=0)])
    sums = group_sum(sums, "grp")
    token_mean = sums[0] / all_chans
    inv_std = lax.rsqrt(sums[1] / all_chans - token_mean * token_mean + norm_eps)
    normed = (tok_val - token_mean) * inv_std
    normal_out = normed * gain[:, None, None] + shift[:, None, None]
    send_field, grad_val = lax.optimization_barrier((lon_parts(normal_out, exact), grad_val))
    recv_field = swap(send_field)
    recv_grad = swap(lon_parts(grad_val, precise))

    mat_in, mat_out = mix_matrix(w_in[0]), mix_matrix(w_out[0])
    at_mode = lax.axis_index("lat") * own + jnp.arange(own)
    mode_weight = jnp.where(at_mode == 0, 1.0, 2.0).astype(jnp.float32)[None, :, None, None]
    spec = lat_in(recv_field, exact)
    pre = contract("kmic,icjo->kmjo", spec, mat_in, exact) + b_in[0]
    act = jax.nn.relu(pre)
    post = contract("kmic,icjo->kmjo", act, mat_out, exact) + b_out[0]
    back_field = lat_out(shrink(post) * mode_weight)
    back_field, spec, pre, act, post, recv_grad = lax.optimization_barrier(
        (back_field, spec, pre, act, post, recv_grad)
    )
    rows_field = swap(back_field)

    grad = lat_in(recv_grad, precise) * mode_weight
    d_post = jnp.where(jnp.abs(post) > shrink_level, grad, 0.0)
    d_act = contract("kmjo,icjo->kmic", d_post, mat_out)
    d_pre = jnp.where(pre > 0.0, d_act, 0.0)
    d_spec = contract("kmjo,icjo->kmic", d_pre, mat_in)
    back_grad, spec, act, d_post, d_pre = lax.optimization_barrier(
        (lat_out(d_spec), spec, act, d_post, d_pre)
    )
    rows_grad = swap(back_grad)
    full_out = contract("kmic,kmjo->icjo", act, d_post)
    full_in = contract("kmic,kmjo->icjo", spec, d_pre)
    grads = jnp.stack([*matrix_grad(full_in), *matrix_grad(full_out)])
    grads = grads.reshape(lat_count, -1) * (1.0 / math.sqrt(lat_len * modes))
    grad_weights = scatter_sum(grads, "lat")

    mixed = (lon_back(rows_field) + normal_out + tok_val).astype(jnp.bfloat16)
    dnorm = (grad_val + lon_back(rows_grad)) * gain[:, None, None]
    back = group_sum(jnp.stack([jnp.sum(dnorm, axis=0), jnp.sum(dnorm * normed, axis=0)]), "grp")
    grad_tokens = grad_val + inv_std * (
        dnorm - back[0] / all_chans - normed * (back[1] / all_chans)
    )
    return (mixed, grad_tokens.astype(jnp.bfloat16), grad_weights)


MESH = pl.DeviceIdType.MESH


def flip(value, half):
    return pltpu.roll(value, half, value.ndim - 1)


def rotate(value, step, count, sense, sign, half):
    step = step % count
    if step == 0:
        return value
    if 2 * step == count:
        return -value
    angle = sense * 2.0 * math.pi * step / count
    turned = sign * flip(value, half)
    if 4 * step == count or 4 * step == 3 * count:
        return turned if math.sin(angle) > 0 else -turned
    return value * math.cos(angle) + turned * math.sin(angle)


def butterflies(values, sense, sign, half):
    count = len(values)
    if count == 1:
        return values
    even = butterflies(values[0::2], sense, sign, half)
    odd = butterflies(values[1::2], sense, sign, half)
    low, high = [], []
    for at in range(count // 2):
        turned = rotate(odd[at], at, count, sense, sign, half)
        low.append(even[at] + turned)
        high.append(even[at] - turned)
    return low + high


def dot(left, right):
    return lax.dot_general(
        left, right, (((1,), (0,)), ((), ())), preferred_element_type=jnp.float32
    )


def dot_lanes(left, right):
    return lax.dot_general(
        left, right, (((1,), (1,)), ((), ())), preferred_element_type=jnp.float32
    )


def halves(value):
    high = value.astype(jnp.bfloat16)
    return high, (value - high.astype(jnp.float32)).astype(jnp.bfloat16)


def band_kernel(
    lat_count, grp_count,
    tok_hbm, cot_hbm, high_hbm, low_hbm, back_hbm, gain, shift, w_in_hbm, b_in_hbm, w_out_hbm, b_out_hbm,
    norm_high, norm_low, gw_out,
    tok, cot, high_tab, low_tab, back_tab,
    f1_send, f1_recv, f2_send, f2_recv, b1_send, b1_recv, b2_send, b2_recv,
    spec, act, shrunk, gspec, work, stats, sum_send, sum_recv,
    mix_in, mix_out, pull_in, pull_out, bias_in, bias_out, acc_in, acc_out,
    gw_send, gw_recv, w_in, b_in, w_out, b_out, send_sem, recv_sem, load_sem,
):
    me, grp = lax.axis_index("lat"), lax.axis_index("grp")
    modes_all, chans, lanes = spec.shape
    half = lanes // 2
    all_rows, length = tok.shape
    rows = all_rows // chans
    chunks = length // lanes
    all_chans = chans * grp_count
    group = 16 // rows if rows < 16 else 1
    tile = group * rows
    piece_rows = 128
    strip = 256
    strips = all_rows // strip
    octets = strip // rows // 8
    extra = 4 * lat_count * strips

    def partner(step):
        other, bit = me, 1
        while bit < lat_count:
            if step & bit:
                other = other + bit * (1 - 2 * lax.rem(lax.div(me, bit), 2))
            bit *= 2
        return other

    def strip_of(at):
        return pl.ds(pl.multiple_of(at * strip, strip), strip)

    def plan(src, dst, kind, step, at):
        part = strip_of(at)
        place = (kind * lat_count + step) * strips + at
        return pltpu.make_async_remote_copy(
            src_ref=src.at[partner(step), part], dst_ref=dst.at[me, part],
            send_sem=send_sem.at[place], recv_sem=recv_sem.at[place],
            device_id=(partner(step), grp), device_id_type=MESH,
        )

    def load(src, dst, at):
        copy = pltpu.make_async_copy(src, dst, load_sem.at[at])
        copy.start()
        return copy

    far, near = list(range(lat_count // 2, lat_count)), list(range(lat_count // 2 - 1, 0, -1))
    first, held = far[0], far[-1]
    f1_order = b2_order = [*near, *far]
    f2_order = [*near, *far[1:]]
    b1_order = [*near, *far[:-1]]

    load_first = load(high_hbm.at[partner(first)], high_tab.at[partner(first)], 1)
    load_cot = load(cot_hbm, cot, 0)

    barrier = pltpu.get_barrier_semaphore()
    for step in range(1, lat_count):
        pl.semaphore_signal(barrier, inc=1, device_id=(partner(step), grp), device_id_type=MESH)
    for step in range(1, grp_count):
        pl.semaphore_signal(
            barrier, inc=1, device_id=(me, lax.rem(grp + step, grp_count)), device_id_type=MESH
        )

    lane = lax.broadcasted_iota(jnp.int32, (1, lanes), 1)
    real_lane = lane < half
    sign = jnp.where(real_lane, -1.0, 1.0).astype(jnp.float32)
    at_mode = jnp.where(real_lane, lane, lane - half) + me * half
    mode_weight = jnp.where(at_mode == 0, 1.0, 2.0).astype(jnp.float32)
    norm = 1.0 / math.sqrt(modes_all)

    def lon(dst, d, at, left_high, left_low, full=True):
        part = strip_of(at)
        out = dot(left_high[part, :], high_tab[d])
        if left_low is not None:
            out = out + dot(left_low[part, :], high_tab[d])
        if full:
            out = out + dot(left_high[part, :], low_tab[d])
        dst[d, part, :] = out

    def group_exchange(use):
        copies = []
        for step in range(1, grp_count):
            copy = pltpu.make_async_remote_copy(
                src_ref=sum_send.at[use], dst_ref=sum_recv.at[use, step],
                send_sem=send_sem.at[extra + use * lat_count + step],
                recv_sem=recv_sem.at[extra + use * lat_count + step],
                device_id=(me, lax.rem(grp + step, grp_count)), device_id_type=MESH,
            )
            copy.start()
            copies.append(copy)
        return copies

    def group_total(use, copies, at):
        for copy in copies:
            copy.wait_recv()
        total = sum_send[use, at]
        for step in range(1, grp_count):
            total = total + sum_recv[use, step, at]
        return total

    load_first.wait()
    load_cot.wait()
    load_tok = load(tok_hbm, tok, 2)
    weight_loads = [
        load(w_in_hbm, w_in, 5), load(b_in_hbm, b_in, 6),
        load(w_out_hbm, w_out, 7), load(b_out_hbm, b_out, 8 + first),
    ]

    def head(at, carry):
        lon(f2_send, partner(first), at, cot, None, False)
        return carry

    lax.fori_loop(0, strips, head, 0)
    pl.semaphore_wait(barrier, lat_count - 1 + grp_count - 1)
    for at in range(strips):
        plan(f2_send, f2_recv, 1, first, at).start()

    load_tok.wait()
    table_loads = {}
    for step in f2_order + [0]:
        d = partner(step)
        table_loads[step] = load(high_hbm.at[d], high_tab.at[d], 8 + step)
    load_low = load(low_hbm, low_tab, 3)

    def sums(at, carry):
        one, two = carry
        part = tok[pl.ds(pl.multiple_of(at * tile, tile), tile), :].astype(jnp.float32)
        for item in range(group):
            value = part[item * rows:(item + 1) * rows, :]
            one, two = one + value, two + value * value
        return one, two

    zero = jnp.zeros((rows, length), jnp.float32)
    one, two = lax.fori_loop(0, all_rows // tile, sums, (zero, zero))
    sum_send[0, 0], sum_send[0, 1] = one, two
    stat_copies = group_exchange(0)

    def prepare(weight, bias, mix, pull, bias_to):
        real_part, imag_part = weight[0, 0], weight[0, 1]
        forward = jnp.concatenate([real_part, imag_part], axis=0).T
        high, low = halves(forward)
        mix[:chans], mix[chans:] = high, low
        backward = jnp.concatenate([real_part.T, imag_part.T], axis=0).T
        high, low = halves(backward)
        pull[:chans], pull[chans:] = high, low
        wide_real = jnp.broadcast_to(bias[0, 0:1, :], (lanes, chans)).T
        wide_imag = jnp.broadcast_to(bias[0, 1:2, :], (lanes, chans)).T
        bias_to[...] = jnp.where(real_lane, wide_real, wide_imag)

    for copy in weight_loads:
        copy.wait()
    prepare(w_in, b_in, mix_in, pull_in, bias_in)
    prepare(w_out, b_out, mix_out, pull_out, bias_out)
    acc_in[...] = jnp.zeros_like(acc_in)
    acc_out[...] = jnp.zeros_like(acc_out)
    for step in f2_order + [0]:
        table_loads[step].wait()
    load_low.wait()

    mean = group_total(0, stat_copies, 0) / all_chans
    square = group_total(0, [], 1) / all_chans
    stats[0] = mean
    stats[1] = lax.rsqrt(square - mean * mean + norm_eps)

    def normal_tile(at):
        part = tok[pl.ds(pl.multiple_of(at * tile, tile), tile), :].astype(jnp.float32)
        normed, normal = [], []
        for item in range(group):
            value = (part[item * rows:(item + 1) * rows, :] - stats[0]) * stats[1]
            normed.append(value)
            normal.append(value * gain[at * group + item] + shift[at * group + item])
        return part, normed, normal

    def normalize(at, carry):
        _, _, normal = normal_tile(at)
        high, low = halves(jnp.concatenate(normal, axis=0))
        part = pl.ds(pl.multiple_of(at * tile, tile), tile)
        norm_high[part, :] = high
        norm_low[part, :] = low
        return carry

    lax.fori_loop(0, all_rows // tile, normalize, 0)

    load_back = load(back_hbm, back_tab, 4)

    def first_strip(at, carry):
        for step in f1_order:
            lon(f1_send, partner(step), at, norm_high, norm_low)
            plan(f1_send, f1_recv, 0, step, at).start()
        lon(f1_recv, me, at, norm_high, norm_low)
        return carry

    lax.fori_loop(0, strips, first_strip, 0)

    def second_strip(at, carry):
        for step in f2_order:
            lon(f2_send, partner(step), at, cot, None)
            plan(f2_send, f2_recv, 1, step, at).start()
        lon(f2_recv, me, at, cot, None)
        return carry

    lax.fori_loop(0, strips, second_strip, 0)

    def lat_forward(src, dst, scale, kind):
        def body(at, carry):
            for row in range(rows):
                values = [
                    src[owner, pl.ds(at * 8 * rows + row, 8, stride=rows), :] * scale
                    for owner in range(lat_count)
                ]
                values = butterflies(values, -1.0, sign, half)
                for low in range(lat_count):
                    work[row * lat_count + low] = rotate(
                        values[low], row * low, modes_all, -1.0, sign, half
                    )
            for low in range(lat_count):
                values = [work[row * lat_count + low] for row in range(rows)]
                values = butterflies(values, -1.0, sign, half)
                for high in range(rows):
                    dst[low + lat_count * high, pl.ds(pl.multiple_of(at * 8, 8), 8), :] = values[high]
            return carry

        def gather(at, carry):
            for step in f1_order:
                plan(src, src, kind, step, at).wait_recv()
            return lax.fori_loop(at * octets, (at + 1) * octets, body, carry)

        lax.fori_loop(0, strips, gather, 0)

    def lat_back(src, dst, scale, kind, to, steps):
        def body(at, carry):
            for low in range(lat_count):
                values = [
                    src[low + lat_count * high, pl.ds(pl.multiple_of(at * 8, 8), 8), :] * scale
                    for high in range(rows)
                ]
                values = butterflies(values, 1.0, sign, half)
                for row in range(rows):
                    work[row * lat_count + low] = rotate(
                        values[row], row * low, modes_all, 1.0, sign, half
                    )
            for row in range(rows):
                values = [work[row * lat_count + low] for low in range(lat_count)]
                values = butterflies(values, 1.0, sign, half)
                for owner in range(lat_count):
                    dst[owner, pl.ds(at * 8 * rows + row, 8, stride=rows), :] = values[owner]
            return carry

        def scatter(at, carry):
            carry = lax.fori_loop(at * octets, (at + 1) * octets, body, carry)
            for step in steps:
                plan(dst, to, kind, step, at).start()
            return carry

        lax.fori_loop(0, strips, scatter, 0)

    def stacked(pair, turn):
        turned = [turn * flip(value, half) for value in pair]
        return jnp.concatenate(
            [jnp.concatenate(pair, axis=1), jnp.concatenate(turned, axis=1)], axis=0
        )

    def mixed_by(matrix, value):
        high, low = halves(value)
        both = dot(matrix[...], high)
        return both[:chans] + both[chans:] + dot(matrix[:chans], low)

    lat_forward(f1_recv, spec, norm, 0)

    def filter_modes(at, carry):
        pair = [spec[2 * at], spec[2 * at + 1]]
        pre = mixed_by(mix_in, stacked(pair, sign))
        pair = []
        for item in range(2):
            value = jnp.maximum(pre[:, item * lanes:(item + 1) * lanes] + bias_in[...], 0.0)
            act[2 * at + item] = value
            pair.append(value)
        post = mixed_by(mix_out, stacked(pair, sign))
        for item in range(2):
            value = post[:, item * lanes:(item + 1) * lanes] + bias_out[...]
            kept = jnp.maximum(jnp.abs(value) - shrink_level, 0.0)
            shrunk[2 * at + item] = jnp.where(value < 0.0, -kept, kept)
        return carry

    lax.fori_loop(0, modes_all // 2, filter_modes, 0)
    lat_back(shrunk, b1_send, norm * mode_weight, 2, b1_recv, b1_order)
    lat_forward(f2_recv, gspec, norm * mode_weight, 1)

    def pull_modes(at, carry):
        pair = []
        for item in range(2):
            pair.append(jnp.where(shrunk[2 * at + item] != 0.0, gspec[2 * at + item], 0.0))
        d_post = stacked(pair, -sign).astype(jnp.bfloat16)
        both = dot(pull_out[...], d_post)
        d_act = both[:chans] + both[chans:]
        acts = [act[2 * at], act[2 * at + 1]]
        high, low = halves(jnp.concatenate(acts, axis=1))
        acc_out[...] += dot_lanes(high, d_post) + dot_lanes(low, d_post)
        pair = []
        for item in range(2):
            value = d_act[:, item * lanes:(item + 1) * lanes]
            pair.append(jnp.where(acts[item] > 0.0, value, 0.0))
        d_pre = stacked(pair, -sign).astype(jnp.bfloat16)
        both = dot(pull_in[...], d_pre)
        d_spec = both[:chans] + both[chans:]
        high, low = halves(jnp.concatenate([spec[2 * at], spec[2 * at + 1]], axis=1))
        acc_in[...] += dot_lanes(high, d_pre) + dot_lanes(low, d_pre)
        for item in range(2):
            gspec[2 * at + item] = d_spec[:, item * lanes:(item + 1) * lanes]
        return carry

    lax.fori_loop(0, modes_all // 2, pull_modes, 0)
    level = 1.0 / math.sqrt(modes_all * lat_count * half)
    gw_rows = gw_recv.shape[1]
    pieces = [acc_in[:, :chans], acc_in[:, chans:], acc_out[:, :chans], acc_out[:, chans:]]
    for at, piece in enumerate(pieces):
        for row in range(0, chans, gw_rows):
            place = (at * chans + row) // gw_rows
            gw_send[place, :, :chans] = piece[row:row + gw_rows, :] * level
    gw = {}
    for step in b2_order:
        gw[step] = pltpu.make_async_remote_copy(
            src_ref=gw_send.at[partner(step)], dst_ref=gw_recv.at[step],
            send_sem=send_sem.at[extra + 2 * lat_count + step],
            recv_sem=recv_sem.at[extra + 2 * lat_count + step],
            device_id=(partner(step), grp), device_id_type=MESH,
        )
        gw[step].start()

    lat_back(gspec, b2_send, norm, 3, b2_recv, b2_order)
    last = []
    for at in range(all_rows // piece_rows):
        part = pl.ds(at * piece_rows, piece_rows)
        copy = pltpu.make_async_remote_copy(
            src_ref=b1_send.at[partner(held), part], dst_ref=b1_recv.at[me, part],
            send_sem=send_sem.at[extra + 3 * lat_count + at],
            recv_sem=recv_sem.at[extra + 3 * lat_count + at],
            device_id=(partner(held), grp), device_id_type=MESH,
        )
        copy.start()
        last.append(copy)

    def lon_back_part(acc, blocks, part, start):
        lefts = [(block[d, part, :].astype(jnp.bfloat16), d) for block, d in blocks]
        for chunk in range(0, chunks, 2):
            columns = slice(chunk * lanes, (chunk + 2) * lanes)
            out = dot(lefts[0][0], back_tab[lefts[0][1], :, columns])
            for left, d in lefts[1:]:
                out = out + dot(left, back_tab[d, :, columns])
            for item in range(2):
                value = out[:, item * lanes:(item + 1) * lanes]
                if not start:
                    value = value + acc[chunk + item, part, :]
                acc[chunk + item, part, :] = value

    def lon_back(acc, sent, got, kind, steps):
        blocks = [(sent, me)] + [(got, partner(step)) for step in steps]

        def piece(at, carry):
            part = pl.ds(pl.multiple_of(at * piece_rows, piece_rows), piece_rows)
            lon_back_part(acc, blocks, part, True)
            return carry

        def body(at, carry):
            for step in steps:
                plan(got, got, kind, step, at).wait_recv()
            count = strip // piece_rows
            return lax.fori_loop(at * count, (at + 1) * count, piece, carry)

        lax.fori_loop(0, strips, body, 0)

    load_back.wait()
    field, pulled = f1_recv, f2_recv
    lon_back(field, b1_send, b1_recv, 2, b1_order)
    lon_back(pulled, b2_send, b2_recv, 3, b2_order)

    def gathered(acc, at):
        part = pl.ds(pl.multiple_of(at * tile, tile), tile)
        return jnp.concatenate([acc[chunk, part, :] for chunk in range(chunks)], axis=1)

    def dnorm_tile(at):
        part, normed, _ = normal_tile(at)
        grad = cot[pl.ds(pl.multiple_of(at * tile, tile), tile), :].astype(jnp.float32)
        whole = grad + gathered(pulled, at)
        dnorm = [
            whole[item * rows:(item + 1) * rows, :] * gain[at * group + item]
            for item in range(group)
        ]
        return grad, normed, dnorm

    def back_sums(at, carry):
        one, two = carry
        _, normed, dnorm = dnorm_tile(at)
        for item in range(group):
            one, two = one + dnorm[item], two + dnorm[item] * normed[item]
        return one, two

    one, two = lax.fori_loop(0, all_rows // tile, back_sums, (zero, zero))
    sum_send[1, 0], sum_send[1, 1] = one, two
    back_copies = group_exchange(1)
    stats[2] = group_total(1, back_copies, 0) / all_chans
    stats[3] = group_total(1, [], 1) / all_chans

    def finish_grad(at, carry):
        grad, normed, dnorm = dnorm_tile(at)
        out = []
        for item in range(group):
            inner = dnorm[item] - stats[2] - normed[item] * stats[3]
            out.append(grad[item * rows:(item + 1) * rows, :] + stats[1] * inner)
        part = pl.ds(pl.multiple_of(at * tile, tile), tile)
        norm_low[part, :] = jnp.concatenate(out, axis=0).astype(jnp.bfloat16)
        return carry

    lax.fori_loop(0, all_rows // tile, finish_grad, 0)

    total = gw_send[me]
    for step in b2_order:
        gw[step].wait_recv()
        total = total + gw_recv[step]
    gw_out[...] = total[:, :chans]

    def finish_mixed(at, carry):
        part, _, normal = normal_tile(at)
        out = gathered(field, at) + jnp.concatenate(normal, axis=0) + part
        norm_high[pl.ds(pl.multiple_of(at * tile, tile), tile), :] = out.astype(jnp.bfloat16)
        return carry

    for at, copy in enumerate(last):
        copy.wait_recv()
        part = pl.ds(at * piece_rows, piece_rows)
        lon_back_part(field, [(b1_recv, partner(held))], part, False)
        tiles = piece_rows // tile
        lax.fori_loop(at * tiles, (at + 1) * tiles, finish_mixed, 0)

    def sent(at, carry):
        for step in b2_order:
            plan(f1_send, f1_recv, 0, step, at).wait_send()
            plan(f2_send, f2_recv, 1, step, at).wait_send()
            plan(b2_send, b2_recv, 3, step, at).wait_send()
        for step in b1_order:
            plan(b1_send, b1_recv, 2, step, at).wait_send()
        return carry

    lax.fori_loop(0, strips, sent, 0)
    for step in b2_order:
        gw[step].wait_send()
    for copy in stat_copies + back_copies + last:
        copy.wait_send()


def fused(lat_count, grp_count, tokens, cotangent, gain, shift, w_in, b_in, w_out, b_out):
    chans, rows, length = tokens.shape
    modes = length // 2
    lanes = 2 * (modes // lat_count)
    lat_len = rows * lat_count
    all_rows = chans * rows
    table = lon_table(length, modes, lat_count).transpose(1, 0, 2, 3)
    table = table.reshape(lat_count, length, lanes)
    high = table.astype(ml_dtypes.bfloat16)
    low = (table - high.astype(np.float32)).astype(ml_dtypes.bfloat16)
    back = np.ascontiguousarray(high.transpose(0, 2, 1))
    gw_rows = 4 * chans // lat_count
    copies = (4 * (all_rows // 256) + 3) * lat_count + all_rows // 128
    f32, bf16 = jnp.float32, jnp.bfloat16
    block = pltpu.VMEM((lat_count, all_rows, lanes), f32)
    modal = pltpu.VMEM((lat_len, chans, lanes), f32)
    anywhere = pl.BlockSpec(memory_space=pl.ANY)
    scalars = pl.BlockSpec(memory_space=pltpu.SMEM)
    inside = pl.BlockSpec(memory_space=pltpu.VMEM)
    mixed, gtok, gw = pl.pallas_call(
        functools.partial(band_kernel, lat_count, grp_count),
        out_shape=(
            pltpu.VMEM((all_rows, length), bf16),
            pltpu.VMEM((all_rows, length), bf16),
            pltpu.VMEM((gw_rows, chans), f32),
        ),
        in_specs=[anywhere] * 5 + [scalars] * 2 + [anywhere] * 4,
        out_specs=(inside, inside, inside),
        scratch_shapes=[
            pltpu.VMEM((all_rows, length), bf16),
            pltpu.VMEM((all_rows, length), bf16),
            pltpu.VMEM((lat_count, length, lanes), bf16),
            pltpu.VMEM((lat_count, length, lanes), bf16),
            pltpu.VMEM((lat_count, lanes, length), bf16),
            *[block] * 8,
            *[modal] * 4,
            pltpu.VMEM((lat_len, 8, lanes), f32),
            pltpu.VMEM((4, rows, length), f32),
            pltpu.VMEM((2, 2, rows, length), f32),
            pltpu.VMEM((2, grp_count, 2, rows, length), f32),
            *[pltpu.VMEM((2 * chans, 2 * chans), bf16)] * 4,
            *[pltpu.VMEM((chans, lanes), f32)] * 2,
            *[pltpu.VMEM((chans, 2 * chans), f32)] * 2,
            pltpu.VMEM((lat_count, gw_rows, lanes), f32),
            pltpu.VMEM((lat_count, gw_rows, lanes), f32),
            *[pltpu.VMEM(value.shape, f32) for value in (w_in, b_in, w_out, b_out)],
            pltpu.SemaphoreType.DMA((copies,)),
            pltpu.SemaphoreType.DMA((copies,)),
            pltpu.SemaphoreType.DMA((8 + lat_count,)),
        ],
        compiler_params=pltpu.CompilerParams(
            collective_id=0, has_side_effects=True, vmem_limit_bytes=56 << 20
        ),
    )(
        tokens.reshape(all_rows, length), cotangent.reshape(all_rows, length),
        jnp.asarray(high), jnp.asarray(low), jnp.asarray(back),
        gain, shift, w_in, b_in, w_out, b_out,
    )
    return (
        mixed.reshape(chans, rows, length), gtok.reshape(chans, rows, length), gw.reshape(1, -1)
    )


def fits(lat_count, grp_count, tokens):
    chans, rows, length = tokens.shape
    lanes = length // lat_count
    gw_rows = 4 * chans // lat_count
    return (
        lanes == 128 and lat_count & (lat_count - 1) == 0 and rows == 8
        and grp_count <= lat_count and chans % gw_rows == 0 and gw_rows % 8 == 0
        and (chans * rows) % 256 == 0 and chans % 16 == 0 and chans <= lanes
    )


def per_part(*args):
    lat_count, grp_count = lax.axis_size("lat"), lax.axis_size("grp")
    if fits(lat_count, grp_count, args[0]):
        return fused(lat_count, grp_count, *args)
    return per_device(*args)


def solution(mesh):
    in_specs = (
        P("grp", "lat", None),
        P("grp", "lat", None),
        P("grp"),
        P("grp"),
        P("grp", None, None, None),
        P("grp", None, None),
        P("grp", None, None, None),
        P("grp", None, None),
    )
    out_specs = (P("grp", "lat", None), P("grp", "lat", None), P("grp", "lat"))
    return jax.shard_map(
        per_part, mesh=mesh, in_specs=in_specs, out_specs=out_specs, check_vma=False
    )
```

```python
import functools
import math

import numpy as np
import ml_dtypes
import jax
import jax.numpy as jnp
from jax import lax
from jax.experimental import pallas as pl
from jax.experimental.pallas import tpu as pltpu
from jax.sharding import PartitionSpec as P

shrink_level = 0.01
norm_eps = 1e-05


precise = lax.Precision.HIGH
exact = lax.Precision.HIGHEST


def contract(form, left, right, level=precise):
    return jnp.einsum(form, left, right, precision=level, preferred_element_type=jnp.float32)


def angles(left_count, right_count, length):
    phase = np.arange(left_count)[:, None] * np.arange(right_count)[None, :] % length
    theta = phase * (2.0 * math.pi / length)
    return np.cos(theta), np.sin(theta)


def lon_table(length, modes, owners):
    cos_tab, sin_tab = angles(length, modes, length)
    both = np.stack([cos_tab, -sin_tab]) / math.sqrt(length)
    both = both.reshape(2, length, owners, modes // owners)
    return both.transpose(1, 2, 0, 3).astype(np.float32)


def lat_table(length):
    cos_tab, sin_tab = angles(length, length, length)
    table = np.stack([np.stack([cos_tab, -sin_tab]), np.stack([sin_tab, cos_tab])])
    return (table / math.sqrt(length)).transpose(2, 0, 3, 1).astype(np.float32)


def group_sum(value, name):
    count = lax.axis_size(name)
    total = value
    for step in range(1, count):
        pairs = [(at, (at + step) % count) for at in range(count)]
        total = total + lax.ppermute(value, name, pairs)
    return total


def scatter_sum(pieces, name):
    count = lax.axis_size(name)
    own = lax.axis_index(name)
    total = lax.dynamic_slice_in_dim(pieces, own, 1, axis=0)
    for step in range(1, count):
        pairs = [(at, (at + step) % count) for at in range(count)]
        piece = lax.dynamic_slice_in_dim(pieces, (own + step) % count, 1, axis=0)
        total = total + lax.ppermute(piece, name, pairs)
    return total


def swap(value):
    return lax.all_to_all(value, "lat", split_axis=0, concat_axis=0, tiled=True)


def mix_matrix(weight):
    real_part, imag_part = weight[0], weight[1]
    top = jnp.stack([real_part, imag_part], axis=1)
    low = jnp.stack([-imag_part, real_part], axis=1)
    return jnp.stack([top, low])


def shrink(value):
    return jnp.sign(value) * jnp.maximum(jnp.abs(value) - shrink_level, 0.0)


def matrix_grad(full):
    real_part = full[0, :, 0] + full[1, :, 1]
    imag_part = full[0, :, 1] - full[1, :, 0]
    return real_part, imag_part


def per_device(tokens, cotangent, gain, shift, w_in, b_in, w_out, b_out):
    chans, rows, length = tokens.shape
    lat_count = lax.axis_size("lat")
    all_chans = chans * lax.axis_size("grp")
    modes = length // 2
    own = modes // lat_count
    lat_len = rows * lat_count
    table = lon_table(length, modes, lat_count).reshape(length, 2 * modes)
    table = jnp.asarray(table)
    lat_tab = jnp.asarray(lat_table(lat_len)).reshape(lat_count, rows, 2, lat_len, 2)
    tok_val = tokens.astype(jnp.float32)
    grad_val = cotangent.astype(jnp.float32)

    def lon_parts(field, level):
        out = contract("crn,ndq->dcrq", field, table.reshape(length, lat_count, 2 * own), level)
        return out.reshape(lat_count, chans * rows, 2 * own)

    def lat_in(parts, level):
        parts = parts.reshape(lat_count, chans, rows, 2, own)
        return contract("scrim,srikj->kmjc", parts, lat_tab, level)

    def lat_out(value):
        out = contract("kmjc,srikj->scrim", value, lat_tab)
        return out.reshape(lat_count, chans * rows, 2 * own)

    def lon_back(parts):
        parts = parts.reshape(lat_count, chans, rows, 2 * own)
        return contract("dcrq,ndq->crn", parts, table.reshape(length, lat_count, 2 * own))

    sums = jnp.stack([jnp.sum(tok_val, axis=0), jnp.sum(tok_val * tok_val, axis=0)])
    sums = group_sum(sums, "grp")
    token_mean = sums[0] / all_chans
    inv_std = lax.rsqrt(sums[1] / all_chans - token_mean * token_mean + norm_eps)
    normed = (tok_val - token_mean) * inv_std
    normal_out = normed * gain[:, None, None] + shift[:, None, None]
    send_field, grad_val = lax.optimization_barrier((lon_parts(normal_out, exact), grad_val))
    recv_field = swap(send_field)
    recv_grad = swap(lon_parts(grad_val, precise))

    mat_in, mat_out = mix_matrix(w_in[0]), mix_matrix(w_out[0])
    at_mode = lax.axis_index("lat") * own + jnp.arange(own)
    mode_weight = jnp.where(at_mode == 0, 1.0, 2.0).astype(jnp.float32)[None, :, None, None]
    spec = lat_in(recv_field, exact)
    pre = contract("kmic,icjo->kmjo", spec, mat_in, exact) + b_in[0]
    act = jax.nn.relu(pre)
    post = contract("kmic,icjo->kmjo", act, mat_out, exact) + b_out[0]
    back_field = lat_out(shrink(post) * mode_weight)
    back_field, spec, pre, act, post, recv_grad = lax.optimization_barrier(
        (back_field, spec, pre, act, post, recv_grad)
    )
    rows_field = swap(back_field)

    grad = lat_in(recv_grad, precise) * mode_weight
    d_post = jnp.where(jnp.abs(post) > shrink_level, grad, 0.0)
    d_act = contract("kmjo,icjo->kmic", d_post, mat_out)
    d_pre = jnp.where(pre > 0.0, d_act, 0.0)
    d_spec = contract("kmjo,icjo->kmic", d_pre, mat_in)
    back_grad, spec, act, d_post, d_pre = lax.optimization_barrier(
        (lat_out(d_spec), spec, act, d_post, d_pre)
    )
    rows_grad = swap(back_grad)
    full_out = contract("kmic,kmjo->icjo", act, d_post)
    full_in = contract("kmic,kmjo->icjo", spec, d_pre)
    grads = jnp.stack([*matrix_grad(full_in), *matrix_grad(full_out)])
    grads = grads.reshape(lat_count, -1) * (1.0 / math.sqrt(lat_len * modes))
    grad_weights = scatter_sum(grads, "lat")

    mixed = (lon_back(rows_field) + normal_out + tok_val).astype(jnp.bfloat16)
    dnorm = (grad_val + lon_back(rows_grad)) * gain[:, None, None]
    back = group_sum(jnp.stack([jnp.sum(dnorm, axis=0), jnp.sum(dnorm * normed, axis=0)]), "grp")
    grad_tokens = grad_val + inv_std * (
        dnorm - back[0] / all_chans - normed * (back[1] / all_chans)
    )
    return (mixed, grad_tokens.astype(jnp.bfloat16), grad_weights)


MESH = pl.DeviceIdType.MESH


def flip(value, half):
    return pltpu.roll(value, half, value.ndim - 1)


def rotate(value, step, count, sense, sign, half):
    step = step % count
    if step == 0:
        return value
    if 2 * step == count:
        return -value
    angle = sense * 2.0 * math.pi * step / count
    turned = sign * flip(value, half)
    if 4 * step == count or 4 * step == 3 * count:
        return turned if math.sin(angle) > 0 else -turned
    return value * math.cos(angle) + turned * math.sin(angle)


def butterflies(values, sense, sign, half):
    count = len(values)
    if count == 1:
        return values
    even = butterflies(values[0::2], sense, sign, half)
    odd = butterflies(values[1::2], sense, sign, half)
    low, high = [], []
    for at in range(count // 2):
        turned = rotate(odd[at], at, count, sense, sign, half)
        low.append(even[at] + turned)
        high.append(even[at] - turned)
    return low + high


def dot(left, right):
    return lax.dot_general(
        left, right, (((1,), (0,)), ((), ())), preferred_element_type=jnp.float32
    )


def dot_lanes(left, right):
    return lax.dot_general(
        left, right, (((1,), (1,)), ((), ())), preferred_element_type=jnp.float32
    )


def halves(value):
    high = value.astype(jnp.bfloat16)
    return high, (value - high.astype(jnp.float32)).astype(jnp.bfloat16)


def band_kernel(
    lat_count, grp_count,
    tok_hbm, cot_hbm, high_hbm, low_hbm, back_hbm, gain, shift, w_in_hbm, b_in_hbm, w_out_hbm, b_out_hbm,
    norm_high, norm_low, gw_out,
    tok, cot, high_tab, low_tab, back_tab,
    f1_send, f1_recv, f2_send, f2_recv, b1_send, b1_recv, b2_send, b2_recv,
    spec, act, shrunk, gspec, work, stats, sum_send, sum_recv,
    mix_in, mix_out, pull_in, pull_out, bias_in, bias_out, acc_in, acc_out,
    gw_send, gw_recv, w_in, b_in, w_out, b_out, send_sem, recv_sem, load_sem,
):
    me, grp = lax.axis_index("lat"), lax.axis_index("grp")
    modes_all, chans, lanes = spec.shape
    half = lanes // 2
    all_rows, length = tok.shape
    rows = all_rows // chans
    chunks = length // lanes
    all_chans = chans * grp_count
    group = 16 // rows if rows < 16 else 1
    tile = group * rows
    piece_rows = 128
    strip = 256
    strips = all_rows // strip
    octets = strip // rows // 8
    extra = 4 * lat_count * strips

    def partner(step):
        other, bit = me, 1
        while bit < lat_count:
            if step & bit:
                other = other + bit * (1 - 2 * lax.rem(lax.div(me, bit), 2))
            bit *= 2
        return other

    def strip_of(at):
        return pl.ds(pl.multiple_of(at * strip, strip), strip)

    def plan(src, dst, kind, step, at):
        part = strip_of(at)
        place = (kind * lat_count + step) * strips + at
        return pltpu.make_async_remote_copy(
            src_ref=src.at[partner(step), part], dst_ref=dst.at[me, part],
            send_sem=send_sem.at[place], recv_sem=recv_sem.at[place],
            device_id=(partner(step), grp), device_id_type=MESH,
        )

    def load(src, dst, at):
        copy = pltpu.make_async_copy(src, dst, load_sem.at[at])
        copy.start()
        return copy

    far, near = list(range(lat_count // 2, lat_count)), list(range(lat_count // 2 - 1, 0, -1))
    first, held = far[0], far[-1]
    f1_order = b2_order = [*near, *far]
    f2_order = [*near, *far[1:]]
    b1_order = [*near, *far[:-1]]

    load_first = load(high_hbm.at[partner(first)], high_tab.at[partner(first)], 1)
    load_cot = load(cot_hbm, cot, 0)

    barrier = pltpu.get_barrier_semaphore()
    for step in range(1, lat_count):
        pl.semaphore_signal(barrier, inc=1, device_id=(partner(step), grp), device_id_type=MESH)
    for step in range(1, grp_count):
        pl.semaphore_signal(
            barrier, inc=1, device_id=(me, lax.rem(grp + step, grp_count)), device_id_type=MESH
        )

    lane = lax.broadcasted_iota(jnp.int32, (1, lanes), 1)
    real_lane = lane < half
    sign = jnp.where(real_lane, -1.0, 1.0).astype(jnp.float32)
    at_mode = jnp.where(real_lane, lane, lane - half) + me * half
    mode_weight = jnp.where(at_mode == 0, 1.0, 2.0).astype(jnp.float32)
    norm = 1.0 / math.sqrt(modes_all)

    def lon(dst, d, at, left_high, left_low, full=True):
        part = strip_of(at)
        out = dot(left_high[part, :], high_tab[d])
        if left_low is not None:
            out = out + dot(left_low[part, :], high_tab[d])
        if full:
            out = out + dot(left_high[part, :], low_tab[d])
        dst[d, part, :] = out

    def group_exchange(use):
        copies = []
        for step in range(1, grp_count):
            copy = pltpu.make_async_remote_copy(
                src_ref=sum_send.at[use], dst_ref=sum_recv.at[use, step],
                send_sem=send_sem.at[extra + use * lat_count + step],
                recv_sem=recv_sem.at[extra + use * lat_count + step],
                device_id=(me, lax.rem(grp + step, grp_count)), device_id_type=MESH,
            )
            copy.start()
            copies.append(copy)
        return copies

    def group_total(use, copies, at):
        for copy in copies:
            copy.wait_recv()
        total = sum_send[use, at]
        for step in range(1, grp_count):
            total = total + sum_recv[use, step, at]
        return total

    load_first.wait()
    load_cot.wait()
    load_tok = load(tok_hbm, tok, 2)
    weight_loads = [
        load(w_in_hbm, w_in, 5), load(b_in_hbm, b_in, 6),
        load(w_out_hbm, w_out, 7), load(b_out_hbm, b_out, 8 + first),
    ]

    def head(at, carry):
        lon(f2_send, partner(first), at, cot, None, False)
        return carry

    lax.fori_loop(0, strips, head, 0)
    pl.semaphore_wait(barrier, lat_count - 1 + grp_count - 1)
    for at in range(strips):
        plan(f2_send, f2_recv, 1, first, at).start()

    load_tok.wait()
    table_loads = {}
    for step in f2_order + [0]:
        d = partner(step)
        table_loads[step] = load(high_hbm.at[d], high_tab.at[d], 8 + step)
    load_low = load(low_hbm, low_tab, 3)

    def sums(at, carry):
        one, two = carry
        part = tok[pl.ds(pl.multiple_of(at * tile, tile), tile), :].astype(jnp.float32)
        for item in range(group):
            value = part[item * rows:(item + 1) * rows, :]
            one, two = one + value, two + value * value
        return one, two

    zero = jnp.zeros((rows, length), jnp.float32)
    one, two = lax.fori_loop(0, all_rows // tile, sums, (zero, zero))
    sum_send[0, 0], sum_send[0, 1] = one, two
    stat_copies = group_exchange(0)

    def prepare(weight, bias, mix, pull, bias_to):
        real_part, imag_part = weight[0, 0], weight[0, 1]
        forward = jnp.concatenate([real_part, imag_part], axis=0).T
        high, low = halves(forward)
        mix[:chans], mix[chans:] = high, low
        backward = jnp.concatenate([real_part.T, imag_part.T], axis=0).T
        high, low = halves(backward)
        pull[:chans], pull[chans:] = high, low
        wide_real = jnp.broadcast_to(bias[0, 0:1, :], (lanes, chans)).T
        wide_imag = jnp.broadcast_to(bias[0, 1:2, :], (lanes, chans)).T
        bias_to[...] = jnp.where(real_lane, wide_real, wide_imag)

    for copy in weight_loads:
        copy.wait()
    prepare(w_in, b_in, mix_in, pull_in, bias_in)
    prepare(w_out, b_out, mix_out, pull_out, bias_out)
    acc_in[...] = jnp.zeros_like(acc_in)
    acc_out[...] = jnp.zeros_like(acc_out)
    for step in f2_order + [0]:
        table_loads[step].wait()
    load_low.wait()

    mean = group_total(0, stat_copies, 0) / all_chans
    square = group_total(0, [], 1) / all_chans
    stats[0] = mean
    stats[1] = lax.rsqrt(square - mean * mean + norm_eps)

    def normal_tile(at):
        part = tok[pl.ds(pl.multiple_of(at * tile, tile), tile), :].astype(jnp.float32)
        normed, normal = [], []
        for item in range(group):
            value = (part[item * rows:(item + 1) * rows, :] - stats[0]) * stats[1]
            normed.append(value)
            normal.append(value * gain[at * group + item] + shift[at * group + item])
        return part, normed, normal

    def normalize(at, carry):
        _, _, normal = normal_tile(at)
        high, low = halves(jnp.concatenate(normal, axis=0))
        part = pl.ds(pl.multiple_of(at * tile, tile), tile)
        norm_high[part, :] = high
        norm_low[part, :] = low
        return carry

    lax.fori_loop(0, all_rows // tile, normalize, 0)

    load_back = load(back_hbm, back_tab, 4)

    def first_strip(at, carry):
        for step in f1_order:
            lon(f1_send, partner(step), at, norm_high, norm_low)
            plan(f1_send, f1_recv, 0, step, at).start()
        lon(f1_recv, me, at, norm_high, norm_low)
        return carry

    lax.fori_loop(0, strips, first_strip, 0)

    def second_strip(at, carry):
        for step in f2_order:
            lon(f2_send, partner(step), at, cot, None)
            plan(f2_send, f2_recv, 1, step, at).start()
        lon(f2_recv, me, at, cot, None)
        return carry

    lax.fori_loop(0, strips, second_strip, 0)

    def lat_forward(src, dst, scale, kind):
        def body(at, carry):
            for row in range(rows):
                values = [
                    src[owner, pl.ds(at * 8 * rows + row, 8, stride=rows), :] * scale
                    for owner in range(lat_count)
                ]
                values = butterflies(values, -1.0, sign, half)
                for low in range(lat_count):
                    work[row * lat_count + low] = rotate(
                        values[low], row * low, modes_all, -1.0, sign, half
                    )
            for low in range(lat_count):
                values = [work[row * lat_count + low] for row in range(rows)]
                values = butterflies(values, -1.0, sign, half)
                for high in range(rows):
                    dst[low + lat_count * high, pl.ds(pl.multiple_of(at * 8, 8), 8), :] = values[high]
            return carry

        def gather(at, carry):
            for step in f1_order:
                plan(src, src, kind, step, at).wait_recv()
            return lax.fori_loop(at * octets, (at + 1) * octets, body, carry)

        lax.fori_loop(0, strips, gather, 0)

    def lat_back(src, dst, scale, kind, to, steps):
        def body(at, carry):
            for low in range(lat_count):
                values = [
                    src[low + lat_count * high, pl.ds(pl.multiple_of(at * 8, 8), 8), :] * scale
                    for high in range(rows)
                ]
                values = butterflies(values, 1.0, sign, half)
                for row in range(rows):
                    work[row * lat_count + low] = rotate(
                        values[row], row * low, modes_all, 1.0, sign, half
                    )
            for row in range(rows):
                values = [work[row * lat_count + low] for low in range(lat_count)]
                values = butterflies(values, 1.0, sign, half)
                for owner in range(lat_count):
                    dst[owner, pl.ds(at * 8 * rows + row, 8, stride=rows), :] = values[owner]
            return carry

        def scatter(at, carry):
            carry = lax.fori_loop(at * octets, (at + 1) * octets, body, carry)
            for step in steps:
                plan(dst, to, kind, step, at).start()
            return carry

        lax.fori_loop(0, strips, scatter, 0)

    def stacked(pair, turn):
        turned = [turn * flip(value, half) for value in pair]
        return jnp.concatenate(
            [jnp.concatenate(pair, axis=1), jnp.concatenate(turned, axis=1)], axis=0
        )

    def mixed_by(matrix, value):
        high, low = halves(value)
        both = dot(matrix[...], high)
        return both[:chans] + both[chans:] + dot(matrix[:chans], low)

    lat_forward(f1_recv, spec, norm, 0)

    def filter_modes(at, carry):
        pair = [spec[2 * at], spec[2 * at + 1]]
        pre = mixed_by(mix_in, stacked(pair, sign))
        pair = []
        for item in range(2):
            value = jnp.maximum(pre[:, item * lanes:(item + 1) * lanes] + bias_in[...], 0.0)
            act[2 * at + item] = value
            pair.append(value)
        post = mixed_by(mix_out, stacked(pair, sign))
        for item in range(2):
            value = post[:, item * lanes:(item + 1) * lanes] + bias_out[...]
            kept = jnp.maximum(jnp.abs(value) - shrink_level, 0.0)
            shrunk[2 * at + item] = jnp.where(value < 0.0, -kept, kept)
        return carry

    lax.fori_loop(0, modes_all // 2, filter_modes, 0)
    lat_back(shrunk, b1_send, norm * mode_weight, 2, b1_recv, b1_order)
    lat_forward(f2_recv, gspec, norm * mode_weight, 1)

    def pull_modes(at, carry):
        pair = []
        for item in range(2):
            pair.append(jnp.where(shrunk[2 * at + item] != 0.0, gspec[2 * at + item], 0.0))
        d_post, rest = halves(stacked(pair, -sign))
        both = dot(pull_out[...], d_post)
        d_act = both[:chans] + both[chans:] + dot(pull_out[:chans], rest)
        acts = [act[2 * at], act[2 * at + 1]]
        high, low = halves(jnp.concatenate(acts, axis=1))
        acc_out[...] += dot_lanes(high, d_post) + dot_lanes(low, d_post) + dot_lanes(high, rest)
        pair = []
        for item in range(2):
            value = d_act[:, item * lanes:(item + 1) * lanes]
            pair.append(jnp.where(acts[item] > 0.0, value, 0.0))
        d_pre, rest = halves(stacked(pair, -sign))
        both = dot(pull_in[...], d_pre)
        d_spec = both[:chans] + both[chans:] + dot(pull_in[:chans], rest)
        high, low = halves(jnp.concatenate([spec[2 * at], spec[2 * at + 1]], axis=1))
        acc_in[...] += dot_lanes(high, d_pre) + dot_lanes(low, d_pre) + dot_lanes(high, rest)
        for item in range(2):
            gspec[2 * at + item] = d_spec[:, item * lanes:(item + 1) * lanes]
        return carry

    lax.fori_loop(0, modes_all // 2, pull_modes, 0)
    level = 1.0 / math.sqrt(modes_all * lat_count * half)
    gw_rows = gw_recv.shape[1]
    pieces = [acc_in[:, :chans], acc_in[:, chans:], acc_out[:, :chans], acc_out[:, chans:]]
    for at, piece in enumerate(pieces):
        for row in range(0, chans, gw_rows):
            place = (at * chans + row) // gw_rows
            gw_send[place, :, :chans] = piece[row:row + gw_rows, :] * level
    gw = {}
    for step in b2_order:
        gw[step] = pltpu.make_async_remote_copy(
            src_ref=gw_send.at[partner(step)], dst_ref=gw_recv.at[step],
            send_sem=send_sem.at[extra + 2 * lat_count + step],
            recv_sem=recv_sem.at[extra + 2 * lat_count + step],
            device_id=(partner(step), grp), device_id_type=MESH,
        )
        gw[step].start()

    lat_back(gspec, b2_send, norm, 3, b2_recv, b2_order)
    last = []
    for at in range(all_rows // piece_rows):
        part = pl.ds(at * piece_rows, piece_rows)
        copy = pltpu.make_async_remote_copy(
            src_ref=b1_send.at[partner(held), part], dst_ref=b1_recv.at[me, part],
            send_sem=send_sem.at[extra + 3 * lat_count + at],
            recv_sem=recv_sem.at[extra + 3 * lat_count + at],
            device_id=(partner(held), grp), device_id_type=MESH,
        )
        copy.start()
        last.append(copy)

    def lon_back_part(acc, blocks, part, start):
        lefts = [(block[d, part, :].astype(jnp.bfloat16), d) for block, d in blocks]
        for chunk in range(0, chunks, 2):
            columns = slice(chunk * lanes, (chunk + 2) * lanes)
            out = dot(lefts[0][0], back_tab[lefts[0][1], :, columns])
            for left, d in lefts[1:]:
                out = out + dot(left, back_tab[d, :, columns])
            for item in range(2):
                value = out[:, item * lanes:(item + 1) * lanes]
                if not start:
                    value = value + acc[chunk + item, part, :]
                acc[chunk + item, part, :] = value

    def lon_back(acc, sent, got, kind, steps):
        blocks = [(sent, me)] + [(got, partner(step)) for step in steps]

        def piece(at, carry):
            part = pl.ds(pl.multiple_of(at * piece_rows, piece_rows), piece_rows)
            lon_back_part(acc, blocks, part, True)
            return carry

        def body(at, carry):
            for step in steps:
                plan(got, got, kind, step, at).wait_recv()
            count = strip // piece_rows
            return lax.fori_loop(at * count, (at + 1) * count, piece, carry)

        lax.fori_loop(0, strips, body, 0)

    load_back.wait()
    field, pulled = f1_recv, f2_recv
    lon_back(field, b1_send, b1_recv, 2, b1_order)
    lon_back(pulled, b2_send, b2_recv, 3, b2_order)

    def gathered(acc, at):
        part = pl.ds(pl.multiple_of(at * tile, tile), tile)
        return jnp.concatenate([acc[chunk, part, :] for chunk in range(chunks)], axis=1)

    def dnorm_tile(at):
        part, normed, _ = normal_tile(at)
        grad = cot[pl.ds(pl.multiple_of(at * tile, tile), tile), :].astype(jnp.float32)
        whole = grad + gathered(pulled, at)
        dnorm = [
            whole[item * rows:(item + 1) * rows, :] * gain[at * group + item]
            for item in range(group)
        ]
        return grad, normed, dnorm

    def back_sums(at, carry):
        one, two = carry
        _, normed, dnorm = dnorm_tile(at)
        for item in range(group):
            one, two = one + dnorm[item], two + dnorm[item] * normed[item]
        return one, two

    one, two = lax.fori_loop(0, all_rows // tile, back_sums, (zero, zero))
    sum_send[1, 0], sum_send[1, 1] = one, two
    back_copies = group_exchange(1)
    stats[2] = group_total(1, back_copies, 0) / all_chans
    stats[3] = group_total(1, [], 1) / all_chans

    def finish_grad(at, carry):
        grad, normed, dnorm = dnorm_tile(at)
        out = []
        for item in range(group):
            inner = dnorm[item] - stats[2] - normed[item] * stats[3]
            out.append(grad[item * rows:(item + 1) * rows, :] + stats[1] * inner)
        part = pl.ds(pl.multiple_of(at * tile, tile), tile)
        norm_low[part, :] = jnp.concatenate(out, axis=0).astype(jnp.bfloat16)
        return carry

    lax.fori_loop(0, all_rows // tile, finish_grad, 0)

    total = gw_send[me]
    for step in b2_order:
        gw[step].wait_recv()
        total = total + gw_recv[step]
    for row in range(gw_rows):
        gw_out[:, row * chans:(row + 1) * chans] = total[row:row + 1, :chans]

    def finish_mixed(at, carry):
        part, _, normal = normal_tile(at)
        out = gathered(field, at) + jnp.concatenate(normal, axis=0) + part
        norm_high[pl.ds(pl.multiple_of(at * tile, tile), tile), :] = out.astype(jnp.bfloat16)
        return carry

    for at, copy in enumerate(last):
        copy.wait_recv()
        part = pl.ds(at * piece_rows, piece_rows)
        lon_back_part(field, [(b1_recv, partner(held))], part, False)
        tiles = piece_rows // tile
        lax.fori_loop(at * tiles, (at + 1) * tiles, finish_mixed, 0)

    def sent(at, carry):
        for step in b2_order:
            plan(f1_send, f1_recv, 0, step, at).wait_send()
            plan(f2_send, f2_recv, 1, step, at).wait_send()
            plan(b2_send, b2_recv, 3, step, at).wait_send()
        for step in b1_order:
            plan(b1_send, b1_recv, 2, step, at).wait_send()
        return carry

    lax.fori_loop(0, strips, sent, 0)
    for step in b2_order:
        gw[step].wait_send()
    for copy in stat_copies + back_copies + last:
        copy.wait_send()


def fused(lat_count, grp_count, tokens, cotangent, gain, shift, w_in, b_in, w_out, b_out):
    chans, rows, length = tokens.shape
    modes = length // 2
    lanes = 2 * (modes // lat_count)
    lat_len = rows * lat_count
    all_rows = chans * rows
    table = lon_table(length, modes, lat_count).transpose(1, 0, 2, 3)
    table = table.reshape(lat_count, length, lanes)
    high = table.astype(ml_dtypes.bfloat16)
    low = (table - high.astype(np.float32)).astype(ml_dtypes.bfloat16)
    back = np.ascontiguousarray(high.transpose(0, 2, 1))
    gw_rows = 4 * chans // lat_count
    copies = (4 * (all_rows // 256) + 3) * lat_count + all_rows // 128
    f32, bf16 = jnp.float32, jnp.bfloat16
    block = pltpu.VMEM((lat_count, all_rows, lanes), f32)
    modal = pltpu.VMEM((lat_len, chans, lanes), f32)
    anywhere = pl.BlockSpec(memory_space=pl.ANY)
    scalars = pl.BlockSpec(memory_space=pltpu.SMEM)
    inside = pl.BlockSpec(memory_space=pltpu.VMEM)
    mixed, gtok, gw = pl.pallas_call(
        functools.partial(band_kernel, lat_count, grp_count),
        out_shape=(
            pltpu.VMEM((all_rows, length), bf16),
            pltpu.VMEM((all_rows, length), bf16),
            pltpu.VMEM((1, gw_rows * chans), f32),
        ),
        in_specs=[anywhere] * 5 + [scalars] * 2 + [anywhere] * 4,
        out_specs=(inside, inside, inside),
        scratch_shapes=[
            pltpu.VMEM((all_rows, length), bf16),
            pltpu.VMEM((all_rows, length), bf16),
            pltpu.VMEM((lat_count, length, lanes), bf16),
            pltpu.VMEM((lat_count, length, lanes), bf16),
            pltpu.VMEM((lat_count, lanes, length), bf16),
            *[block] * 8,
            *[modal] * 4,
            pltpu.VMEM((lat_len, 8, lanes), f32),
            pltpu.VMEM((4, rows, length), f32),
            pltpu.VMEM((2, 2, rows, length), f32),
            pltpu.VMEM((2, grp_count, 2, rows, length), f32),
            *[pltpu.VMEM((2 * chans, 2 * chans), bf16)] * 4,
            *[pltpu.VMEM((chans, lanes), f32)] * 2,
            *[pltpu.VMEM((chans, 2 * chans), f32)] * 2,
            pltpu.VMEM((lat_count, gw_rows, lanes), f32),
            pltpu.VMEM((lat_count, gw_rows, lanes), f32),
            *[pltpu.VMEM(value.shape, f32) for value in (w_in, b_in, w_out, b_out)],
            pltpu.SemaphoreType.DMA((copies,)),
            pltpu.SemaphoreType.DMA((copies,)),
            pltpu.SemaphoreType.DMA((8 + lat_count,)),
        ],
        compiler_params=pltpu.CompilerParams(
            collective_id=0, has_side_effects=True, vmem_limit_bytes=56 << 20
        ),
    )(
        tokens.reshape(all_rows, length), cotangent.reshape(all_rows, length),
        jnp.asarray(high), jnp.asarray(low), jnp.asarray(back),
        gain, shift, w_in, b_in, w_out, b_out,
    )
    return (
        mixed.reshape(chans, rows, length), gtok.reshape(chans, rows, length), gw
    )


def fits(lat_count, grp_count, tokens):
    chans, rows, length = tokens.shape
    lanes = length // lat_count
    gw_rows = 4 * chans // lat_count
    return (
        lanes == 128 and lat_count & (lat_count - 1) == 0 and rows == 8
        and grp_count <= lat_count and chans % gw_rows == 0 and gw_rows % 8 == 0
        and (chans * rows) % 256 == 0 and chans % 16 == 0 and chans <= lanes
    )


def per_part(*args):
    lat_count, grp_count = lax.axis_size("lat"), lax.axis_size("grp")
    if fits(lat_count, grp_count, args[0]):
        return fused(lat_count, grp_count, *args)
    return per_device(*args)


def solution(mesh):
    in_specs = (
        P("grp", "lat", None),
        P("grp", "lat", None),
        P("grp"),
        P("grp"),
        P("grp", None, None, None),
        P("grp", None, None),
        P("grp", None, None, None),
        P("grp", None, None),
    )
    out_specs = (P("grp", "lat", None), P("grp", "lat", None), P("grp", "lat"))
    return jax.shard_map(
        per_part, mesh=mesh, in_specs=in_specs, out_specs=out_specs, check_vma=False
    )
```

```python
import functools
import math

import numpy as np
import ml_dtypes
import jax
import jax.numpy as jnp
from jax import lax
from jax.experimental import pallas as pl
from jax.experimental.pallas import tpu as pltpu
from jax.sharding import PartitionSpec as P

shrink_level = 0.01
norm_eps = 1e-05


precise = lax.Precision.HIGH
exact = lax.Precision.HIGHEST


def contract(form, left, right, level=precise):
    return jnp.einsum(form, left, right, precision=level, preferred_element_type=jnp.float32)


def angles(left_count, right_count, length):
    phase = np.arange(left_count)[:, None] * np.arange(right_count)[None, :] % length
    theta = phase * (2.0 * math.pi / length)
    return np.cos(theta), np.sin(theta)


def lon_table(length, modes, owners):
    cos_tab, sin_tab = angles(length, modes, length)
    both = np.stack([cos_tab, -sin_tab]) / math.sqrt(length)
    both = both.reshape(2, length, owners, modes // owners)
    return both.transpose(1, 2, 0, 3).astype(np.float32)


def lat_table(length):
    cos_tab, sin_tab = angles(length, length, length)
    table = np.stack([np.stack([cos_tab, -sin_tab]), np.stack([sin_tab, cos_tab])])
    return (table / math.sqrt(length)).transpose(2, 0, 3, 1).astype(np.float32)


def group_sum(value, name):
    count = lax.axis_size(name)
    total = value
    for step in range(1, count):
        pairs = [(at, (at + step) % count) for at in range(count)]
        total = total + lax.ppermute(value, name, pairs)
    return total


def scatter_sum(pieces, name):
    count = lax.axis_size(name)
    own = lax.axis_index(name)
    total = lax.dynamic_slice_in_dim(pieces, own, 1, axis=0)
    for step in range(1, count):
        pairs = [(at, (at + step) % count) for at in range(count)]
        piece = lax.dynamic_slice_in_dim(pieces, (own + step) % count, 1, axis=0)
        total = total + lax.ppermute(piece, name, pairs)
    return total


def swap(value):
    return lax.all_to_all(value, "lat", split_axis=0, concat_axis=0, tiled=True)


def mix_matrix(weight):
    real_part, imag_part = weight[0], weight[1]
    top = jnp.stack([real_part, imag_part], axis=1)
    low = jnp.stack([-imag_part, real_part], axis=1)
    return jnp.stack([top, low])


def shrink(value):
    return jnp.sign(value) * jnp.maximum(jnp.abs(value) - shrink_level, 0.0)


def matrix_grad(full):
    real_part = full[0, :, 0] + full[1, :, 1]
    imag_part = full[0, :, 1] - full[1, :, 0]
    return real_part, imag_part


def per_device(tokens, cotangent, gain, shift, w_in, b_in, w_out, b_out):
    chans, rows, length = tokens.shape
    lat_count = lax.axis_size("lat")
    all_chans = chans * lax.axis_size("grp")
    modes = length // 2
    own = modes // lat_count
    lat_len = rows * lat_count
    table = lon_table(length, modes, lat_count).reshape(length, 2 * modes)
    table = jnp.asarray(table)
    lat_tab = jnp.asarray(lat_table(lat_len)).reshape(lat_count, rows, 2, lat_len, 2)
    tok_val = tokens.astype(jnp.float32)
    grad_val = cotangent.astype(jnp.float32)

    def lon_parts(field, level):
        out = contract("crn,ndq->dcrq", field, table.reshape(length, lat_count, 2 * own), level)
        return out.reshape(lat_count, chans * rows, 2 * own)

    def lat_in(parts, level):
        parts = parts.reshape(lat_count, chans, rows, 2, own)
        return contract("scrim,srikj->kmjc", parts, lat_tab, level)

    def lat_out(value):
        out = contract("kmjc,srikj->scrim", value, lat_tab)
        return out.reshape(lat_count, chans * rows, 2 * own)

    def lon_back(parts):
        parts = parts.reshape(lat_count, chans, rows, 2 * own)
        return contract("dcrq,ndq->crn", parts, table.reshape(length, lat_count, 2 * own))

    sums = jnp.stack([jnp.sum(tok_val, axis=0), jnp.sum(tok_val * tok_val, axis=0)])
    sums = group_sum(sums, "grp")
    token_mean = sums[0] / all_chans
    inv_std = lax.rsqrt(sums[1] / all_chans - token_mean * token_mean + norm_eps)
    normed = (tok_val - token_mean) * inv_std
    normal_out = normed * gain[:, None, None] + shift[:, None, None]
    send_field, grad_val = lax.optimization_barrier((lon_parts(normal_out, exact), grad_val))
    recv_field = swap(send_field)
    recv_grad = swap(lon_parts(grad_val, precise))

    mat_in, mat_out = mix_matrix(w_in[0]), mix_matrix(w_out[0])
    at_mode = lax.axis_index("lat") * own + jnp.arange(own)
    mode_weight = jnp.where(at_mode == 0, 1.0, 2.0).astype(jnp.float32)[None, :, None, None]
    spec = lat_in(recv_field, exact)
    pre = contract("kmic,icjo->kmjo", spec, mat_in, exact) + b_in[0]
    act = jax.nn.relu(pre)
    post = contract("kmic,icjo->kmjo", act, mat_out, exact) + b_out[0]
    back_field = lat_out(shrink(post) * mode_weight)
    back_field, spec, pre, act, post, recv_grad = lax.optimization_barrier(
        (back_field, spec, pre, act, post, recv_grad)
    )
    rows_field = swap(back_field)

    grad = lat_in(recv_grad, precise) * mode_weight
    d_post = jnp.where(jnp.abs(post) > shrink_level, grad, 0.0)
    d_act = contract("kmjo,icjo->kmic", d_post, mat_out)
    d_pre = jnp.where(pre > 0.0, d_act, 0.0)
    d_spec = contract("kmjo,icjo->kmic", d_pre, mat_in)
    back_grad, spec, act, d_post, d_pre = lax.optimization_barrier(
        (lat_out(d_spec), spec, act, d_post, d_pre)
    )
    rows_grad = swap(back_grad)
    full_out = contract("kmic,kmjo->icjo", act, d_post)
    full_in = contract("kmic,kmjo->icjo", spec, d_pre)
    grads = jnp.stack([*matrix_grad(full_in), *matrix_grad(full_out)])
    grads = grads.reshape(lat_count, -1) * (1.0 / math.sqrt(lat_len * modes))
    grad_weights = scatter_sum(grads, "lat")

    mixed = (lon_back(rows_field) + normal_out + tok_val).astype(jnp.bfloat16)
    dnorm = (grad_val + lon_back(rows_grad)) * gain[:, None, None]
    back = group_sum(jnp.stack([jnp.sum(dnorm, axis=0), jnp.sum(dnorm * normed, axis=0)]), "grp")
    grad_tokens = grad_val + inv_std * (
        dnorm - back[0] / all_chans - normed * (back[1] / all_chans)
    )
    return (mixed, grad_tokens.astype(jnp.bfloat16), grad_weights)


MESH = pl.DeviceIdType.MESH


def flip(value, half):
    return pltpu.roll(value, half, value.ndim - 1)


def rotate(value, step, count, sense, sign, half):
    step = step % count
    if step == 0:
        return value
    if 2 * step == count:
        return -value
    angle = sense * 2.0 * math.pi * step / count
    turned = sign * flip(value, half)
    if 4 * step == count or 4 * step == 3 * count:
        return turned if math.sin(angle) > 0 else -turned
    return value * math.cos(angle) + turned * math.sin(angle)


def butterflies(values, sense, sign, half):
    count = len(values)
    if count == 1:
        return values
    even = butterflies(values[0::2], sense, sign, half)
    odd = butterflies(values[1::2], sense, sign, half)
    low, high = [], []
    for at in range(count // 2):
        turned = rotate(odd[at], at, count, sense, sign, half)
        low.append(even[at] + turned)
        high.append(even[at] - turned)
    return low + high


def dot(left, right):
    return lax.dot_general(
        left, right, (((1,), (0,)), ((), ())), preferred_element_type=jnp.float32
    )


def dot_lanes(left, right):
    return lax.dot_general(
        left, right, (((1,), (1,)), ((), ())), preferred_element_type=jnp.float32
    )


def halves(value):
    high = value.astype(jnp.bfloat16)
    return high, (value - high.astype(jnp.float32)).astype(jnp.bfloat16)


def band_kernel(
    lat_count, grp_count,
    tok_hbm, cot_hbm, high_hbm, low_hbm, back_hbm, gain, shift, w_in_hbm, b_in_hbm, w_out_hbm, b_out_hbm,
    norm_high, norm_low, gw_out,
    tok, cot, high_tab, low_tab, back_tab,
    f1_send, f1_recv, f2_send, f2_recv, b1_send, b1_recv, b2_send, b2_recv,
    spec, act, shrunk, gspec, work, stats, sum_send, sum_recv,
    mix_in, mix_out, pull_in, pull_out, bias_in, bias_out, acc_in, acc_out,
    gw_send, gw_recv, w_in, b_in, w_out, b_out, send_sem, recv_sem, load_sem,
):
    me, grp = lax.axis_index("lat"), lax.axis_index("grp")
    modes_all, chans, lanes = spec.shape
    half = lanes // 2
    all_rows, length = tok.shape
    rows = all_rows // chans
    chunks = length // lanes
    all_chans = chans * grp_count
    group = 16 // rows if rows < 16 else 1
    tile = group * rows
    piece_rows = 128
    strip = 256
    strips = all_rows // strip
    octets = strip // rows // 8
    extra = 4 * lat_count * strips

    def partner(step):
        other, bit = me, 1
        while bit < lat_count:
            if step & bit:
                other = other + bit * (1 - 2 * lax.rem(lax.div(me, bit), 2))
            bit *= 2
        return other

    def strip_of(at):
        return pl.ds(pl.multiple_of(at * strip, strip), strip)

    def plan(src, dst, kind, step, at):
        part = strip_of(at)
        place = (kind * lat_count + step) * strips + at
        return pltpu.make_async_remote_copy(
            src_ref=src.at[partner(step), part], dst_ref=dst.at[me, part],
            send_sem=send_sem.at[place], recv_sem=recv_sem.at[place],
            device_id=(partner(step), grp), device_id_type=MESH,
        )

    def load(src, dst, at):
        copy = pltpu.make_async_copy(src, dst, load_sem.at[at])
        copy.start()
        return copy

    half_way = lat_count // 2
    far = [*range(half_way, lat_count, 2), *range(half_way + 1, lat_count, 2)]
    near = list(range(half_way - 1, 0, -1))
    first, held = far[0], far[-1]
    f1_order = b2_order = [*near, *far]
    f2_order = [*near, *far[1:]]
    b1_order = [*near, *far[:-1]]

    load_first = load(high_hbm.at[partner(first)], high_tab.at[partner(first)], 1)
    load_cot = load(cot_hbm, cot, 0)

    barrier = pltpu.get_barrier_semaphore()
    for step in range(1, lat_count):
        pl.semaphore_signal(barrier, inc=1, device_id=(partner(step), grp), device_id_type=MESH)
    for step in range(1, grp_count):
        pl.semaphore_signal(
            barrier, inc=1, device_id=(me, lax.rem(grp + step, grp_count)), device_id_type=MESH
        )

    lane = lax.broadcasted_iota(jnp.int32, (1, lanes), 1)
    real_lane = lane < half
    sign = jnp.where(real_lane, -1.0, 1.0).astype(jnp.float32)
    at_mode = jnp.where(real_lane, lane, lane - half) + me * half
    mode_weight = jnp.where(at_mode == 0, 1.0, 2.0).astype(jnp.float32)
    norm = 1.0 / math.sqrt(modes_all)

    def lon(dst, d, at, left_high, left_low, full=True):
        part = strip_of(at)
        out = dot(left_high[part, :], high_tab[d])
        if left_low is not None:
            out = out + dot(left_low[part, :], high_tab[d])
        if full:
            out = out + dot(left_high[part, :], low_tab[d])
        dst[d, part, :] = out

    def group_exchange(use):
        copies = []
        for step in range(1, grp_count):
            copy = pltpu.make_async_remote_copy(
                src_ref=sum_send.at[use], dst_ref=sum_recv.at[use, step],
                send_sem=send_sem.at[extra + use * lat_count + step],
                recv_sem=recv_sem.at[extra + use * lat_count + step],
                device_id=(me, lax.rem(grp + step, grp_count)), device_id_type=MESH,
            )
            copy.start()
            copies.append(copy)
        return copies

    def group_total(use, copies, at):
        for copy in copies:
            copy.wait_recv()
        total = sum_send[use, at]
        for step in range(1, grp_count):
            total = total + sum_recv[use, step, at]
        return total

    load_first.wait()
    load_cot.wait()
    load_tok = load(tok_hbm, tok, 2)
    weight_loads = [
        load(w_in_hbm, w_in, 5), load(b_in_hbm, b_in, 6),
        load(w_out_hbm, w_out, 7), load(b_out_hbm, b_out, 8 + first),
    ]

    def head(at, carry):
        lon(f2_send, partner(first), at, cot, None, False)
        return carry

    lax.fori_loop(0, strips, head, 0)
    pl.semaphore_wait(barrier, lat_count - 1 + grp_count - 1)
    for at in range(strips):
        plan(f2_send, f2_recv, 1, first, at).start()

    load_tok.wait()
    table_loads = {}
    for step in f2_order + [0]:
        d = partner(step)
        table_loads[step] = load(high_hbm.at[d], high_tab.at[d], 8 + step)
    load_low = load(low_hbm, low_tab, 3)

    def sums(at, carry):
        one, two = carry
        part = tok[pl.ds(pl.multiple_of(at * tile, tile), tile), :].astype(jnp.float32)
        for item in range(group):
            value = part[item * rows:(item + 1) * rows, :]
            one, two = one + value, two + value * value
        return one, two

    zero = jnp.zeros((rows, length), jnp.float32)
    one, two = lax.fori_loop(0, all_rows // tile, sums, (zero, zero))
    sum_send[0, 0], sum_send[0, 1] = one, two
    stat_copies = group_exchange(0)

    def prepare(weight, bias, mix, pull, bias_to):
        real_part, imag_part = weight[0, 0], weight[0, 1]
        forward = jnp.concatenate([real_part, imag_part], axis=0).T
        high, low = halves(forward)
        mix[:chans], mix[chans:] = high, low
        backward = jnp.concatenate([real_part.T, imag_part.T], axis=0).T
        high, low = halves(backward)
        pull[:chans], pull[chans:] = high, low
        wide_real = jnp.broadcast_to(bias[0, 0:1, :], (lanes, chans)).T
        wide_imag = jnp.broadcast_to(bias[0, 1:2, :], (lanes, chans)).T
        bias_to[...] = jnp.where(real_lane, wide_real, wide_imag)

    for copy in weight_loads:
        copy.wait()
    prepare(w_in, b_in, mix_in, pull_in, bias_in)
    prepare(w_out, b_out, mix_out, pull_out, bias_out)
    acc_in[...] = jnp.zeros_like(acc_in)
    acc_out[...] = jnp.zeros_like(acc_out)
    for step in f2_order + [0]:
        table_loads[step].wait()
    load_low.wait()

    mean = group_total(0, stat_copies, 0) / all_chans
    square = group_total(0, [], 1) / all_chans
    stats[0] = mean
    stats[1] = lax.rsqrt(square - mean * mean + norm_eps)

    def normal_tile(at):
        part = tok[pl.ds(pl.multiple_of(at * tile, tile), tile), :].astype(jnp.float32)
        normed, normal = [], []
        for item in range(group):
            value = (part[item * rows:(item + 1) * rows, :] - stats[0]) * stats[1]
            normed.append(value)
            normal.append(value * gain[at * group + item] + shift[at * group + item])
        return part, normed, normal

    def normalize(at, carry):
        _, _, normal = normal_tile(at)
        high, low = halves(jnp.concatenate(normal, axis=0))
        part = pl.ds(pl.multiple_of(at * tile, tile), tile)
        norm_high[part, :] = high
        norm_low[part, :] = low
        return carry

    lax.fori_loop(0, all_rows // tile, normalize, 0)

    load_back = load(back_hbm, back_tab, 4)

    def first_strip(at, carry):
        for step in f1_order:
            lon(f1_send, partner(step), at, norm_high, norm_low)
            plan(f1_send, f1_recv, 0, step, at).start()
        lon(f1_recv, me, at, norm_high, norm_low)
        return carry

    lax.fori_loop(0, strips, first_strip, 0)

    def second_strip(at, carry):
        for step in f2_order:
            lon(f2_send, partner(step), at, cot, None)
            plan(f2_send, f2_recv, 1, step, at).start()
        lon(f2_recv, me, at, cot, None)
        return carry

    lax.fori_loop(0, strips, second_strip, 0)

    def lat_forward(src, dst, scale, kind):
        def body(at, carry):
            for row in range(rows):
                values = [
                    src[owner, pl.ds(at * 8 * rows + row, 8, stride=rows), :] * scale
                    for owner in range(lat_count)
                ]
                values = butterflies(values, -1.0, sign, half)
                for low in range(lat_count):
                    work[row * lat_count + low] = rotate(
                        values[low], row * low, modes_all, -1.0, sign, half
                    )
            for low in range(lat_count):
                values = [work[row * lat_count + low] for row in range(rows)]
                values = butterflies(values, -1.0, sign, half)
                for high in range(rows):
                    dst[low + lat_count * high, pl.ds(pl.multiple_of(at * 8, 8), 8), :] = values[high]
            return carry

        def gather(at, carry):
            for step in f1_order:
                plan(src, src, kind, step, at).wait_recv()
            return lax.fori_loop(at * octets, (at + 1) * octets, body, carry)

        lax.fori_loop(0, strips, gather, 0)

    def lat_back(src, dst, scale, kind, to, steps):
        def body(at, carry):
            for low in range(lat_count):
                values = [
                    src[low + lat_count * high, pl.ds(pl.multiple_of(at * 8, 8), 8), :] * scale
                    for high in range(rows)
                ]
                values = butterflies(values, 1.0, sign, half)
                for row in range(rows):
                    work[row * lat_count + low] = rotate(
                        values[row], row * low, modes_all, 1.0, sign, half
                    )
            for row in range(rows):
                values = [work[row * lat_count + low] for low in range(lat_count)]
                values = butterflies(values, 1.0, sign, half)
                for owner in range(lat_count):
                    dst[owner, pl.ds(at * 8 * rows + row, 8, stride=rows), :] = values[owner]
            return carry

        def scatter(at, carry):
            carry = lax.fori_loop(at * octets, (at + 1) * octets, body, carry)
            for step in steps:
                plan(dst, to, kind, step, at).start()
            return carry

        lax.fori_loop(0, strips, scatter, 0)

    def stacked(pair, turn):
        turned = [turn * flip(value, half) for value in pair]
        return jnp.concatenate(
            [jnp.concatenate(pair, axis=1), jnp.concatenate(turned, axis=1)], axis=0
        )

    def mixed_by(matrix, value):
        high, low = halves(value)
        both = dot(matrix[...], high)
        return both[:chans] + both[chans:] + dot(matrix[:chans], low)

    lat_forward(f1_recv, spec, norm, 0)

    def filter_modes(at, carry):
        pair = [spec[2 * at], spec[2 * at + 1]]
        pre = mixed_by(mix_in, stacked(pair, sign))
        pair = []
        for item in range(2):
            value = jnp.maximum(pre[:, item * lanes:(item + 1) * lanes] + bias_in[...], 0.0)
            act[2 * at + item] = value
            pair.append(value)
        post = mixed_by(mix_out, stacked(pair, sign))
        for item in range(2):
            value = post[:, item * lanes:(item + 1) * lanes] + bias_out[...]
            kept = jnp.maximum(jnp.abs(value) - shrink_level, 0.0)
            shrunk[2 * at + item] = jnp.where(value < 0.0, -kept, kept)
        return carry

    lax.fori_loop(0, modes_all // 2, filter_modes, 0)
    lat_back(shrunk, b1_send, norm * mode_weight, 2, b1_recv, b1_order)
    lat_forward(f2_recv, gspec, norm * mode_weight, 1)

    def pull_modes(at, carry):
        pair = []
        for item in range(2):
            pair.append(jnp.where(shrunk[2 * at + item] != 0.0, gspec[2 * at + item], 0.0))
        d_post, rest = halves(stacked(pair, -sign))
        both = dot(pull_out[...], d_post)
        d_act = both[:chans] + both[chans:] + dot(pull_out[:chans], rest)
        acts = [act[2 * at], act[2 * at + 1]]
        high, low = halves(jnp.concatenate(acts, axis=1))
        acc_out[...] += dot_lanes(high, d_post) + dot_lanes(low, d_post) + dot_lanes(high, rest)
        pair = []
        for item in range(2):
            value = d_act[:, item * lanes:(item + 1) * lanes]
            pair.append(jnp.where(acts[item] > 0.0, value, 0.0))
        d_pre, rest = halves(stacked(pair, -sign))
        both = dot(pull_in[...], d_pre)
        d_spec = both[:chans] + both[chans:] + dot(pull_in[:chans], rest)
        high, low = halves(jnp.concatenate([spec[2 * at], spec[2 * at + 1]], axis=1))
        acc_in[...] += dot_lanes(high, d_pre) + dot_lanes(low, d_pre) + dot_lanes(high, rest)
        for item in range(2):
            gspec[2 * at + item] = d_spec[:, item * lanes:(item + 1) * lanes]
        return carry

    lax.fori_loop(0, modes_all // 2, pull_modes, 0)
    level = 1.0 / math.sqrt(modes_all * lat_count * half)
    gw_rows = gw_recv.shape[1]
    pieces = [acc_in[:, :chans], acc_in[:, chans:], acc_out[:, :chans], acc_out[:, chans:]]
    for at, piece in enumerate(pieces):
        for row in range(0, chans, gw_rows):
            place = (at * chans + row) // gw_rows
            gw_send[place, :, :chans] = piece[row:row + gw_rows, :] * level
    gw = {}
    for step in b2_order:
        gw[step] = pltpu.make_async_remote_copy(
            src_ref=gw_send.at[partner(step)], dst_ref=gw_recv.at[step],
            send_sem=send_sem.at[extra + 2 * lat_count + step],
            recv_sem=recv_sem.at[extra + 2 * lat_count + step],
            device_id=(partner(step), grp), device_id_type=MESH,
        )
        gw[step].start()

    lat_back(gspec, b2_send, norm, 3, b2_recv, b2_order)
    last = []
    for at in range(all_rows // piece_rows):
        part = pl.ds(at * piece_rows, piece_rows)
        copy = pltpu.make_async_remote_copy(
            src_ref=b1_send.at[partner(held), part], dst_ref=b1_recv.at[me, part],
            send_sem=send_sem.at[extra + 3 * lat_count + at],
            recv_sem=recv_sem.at[extra + 3 * lat_count + at],
            device_id=(partner(held), grp), device_id_type=MESH,
        )
        copy.start()
        last.append(copy)

    def lon_back_part(acc, blocks, part, start):
        lefts = [(block[d, part, :].astype(jnp.bfloat16), d) for block, d in blocks]
        for chunk in range(0, chunks, 2):
            columns = slice(chunk * lanes, (chunk + 2) * lanes)
            out = dot(lefts[0][0], back_tab[lefts[0][1], :, columns])
            for left, d in lefts[1:]:
                out = out + dot(left, back_tab[d, :, columns])
            for item in range(2):
                value = out[:, item * lanes:(item + 1) * lanes]
                if not start:
                    value = value + acc[chunk + item, part, :]
                acc[chunk + item, part, :] = value

    def lon_back(acc, sent, got, kind, steps):
        blocks = [(sent, me)] + [(got, partner(step)) for step in steps]

        def piece(at, carry):
            part = pl.ds(pl.multiple_of(at * piece_rows, piece_rows), piece_rows)
            lon_back_part(acc, blocks, part, True)
            return carry

        def body(at, carry):
            for step in steps:
                plan(got, got, kind, step, at).wait_recv()
            count = strip // piece_rows
            return lax.fori_loop(at * count, (at + 1) * count, piece, carry)

        lax.fori_loop(0, strips, body, 0)

    load_back.wait()
    field, pulled = f1_recv, f2_recv
    lon_back(field, b1_send, b1_recv, 2, b1_order)
    lon_back(pulled, b2_send, b2_recv, 3, b2_order)

    def gathered(acc, at):
        part = pl.ds(pl.multiple_of(at * tile, tile), tile)
        return jnp.concatenate([acc[chunk, part, :] for chunk in range(chunks)], axis=1)

    def dnorm_tile(at):
        part, normed, _ = normal_tile(at)
        grad = cot[pl.ds(pl.multiple_of(at * tile, tile), tile), :].astype(jnp.float32)
        whole = grad + gathered(pulled, at)
        dnorm = [
            whole[item * rows:(item + 1) * rows, :] * gain[at * group + item]
            for item in range(group)
        ]
        return grad, normed, dnorm

    def back_sums(at, carry):
        one, two = carry
        _, normed, dnorm = dnorm_tile(at)
        for item in range(group):
            one, two = one + dnorm[item], two + dnorm[item] * normed[item]
        return one, two

    one, two = lax.fori_loop(0, all_rows // tile, back_sums, (zero, zero))
    sum_send[1, 0], sum_send[1, 1] = one, two
    back_copies = group_exchange(1)
    stats[2] = group_total(1, back_copies, 0) / all_chans
    stats[3] = group_total(1, [], 1) / all_chans

    def finish_grad(at, carry):
        grad, normed, dnorm = dnorm_tile(at)
        out = []
        for item in range(group):
            inner = dnorm[item] - stats[2] - normed[item] * stats[3]
            out.append(grad[item * rows:(item + 1) * rows, :] + stats[1] * inner)
        part = pl.ds(pl.multiple_of(at * tile, tile), tile)
        norm_low[part, :] = jnp.concatenate(out, axis=0).astype(jnp.bfloat16)
        return carry

    lax.fori_loop(0, all_rows // tile, finish_grad, 0)

    total = gw_send[me]
    for step in b2_order:
        gw[step].wait_recv()
        total = total + gw_recv[step]
    for row in range(gw_rows):
        gw_out[:, row * chans:(row + 1) * chans] = total[row:row + 1, :chans]

    def finish_mixed(at, carry):
        part, _, normal = normal_tile(at)
        out = gathered(field, at) + jnp.concatenate(normal, axis=0) + part
        norm_high[pl.ds(pl.multiple_of(at * tile, tile), tile), :] = out.astype(jnp.bfloat16)
        return carry

    for at, copy in enumerate(last):
        copy.wait_recv()
        part = pl.ds(at * piece_rows, piece_rows)
        lon_back_part(field, [(b1_recv, partner(held))], part, False)
        tiles = piece_rows // tile
        lax.fori_loop(at * tiles, (at + 1) * tiles, finish_mixed, 0)

    def sent(at, carry):
        for step in b2_order:
            plan(f1_send, f1_recv, 0, step, at).wait_send()
            plan(f2_send, f2_recv, 1, step, at).wait_send()
            plan(b2_send, b2_recv, 3, step, at).wait_send()
        for step in b1_order:
            plan(b1_send, b1_recv, 2, step, at).wait_send()
        return carry

    lax.fori_loop(0, strips, sent, 0)
    for step in b2_order:
        gw[step].wait_send()
    for copy in stat_copies + back_copies + last:
        copy.wait_send()


def fused(lat_count, grp_count, tokens, cotangent, gain, shift, w_in, b_in, w_out, b_out):
    chans, rows, length = tokens.shape
    modes = length // 2
    lanes = 2 * (modes // lat_count)
    lat_len = rows * lat_count
    all_rows = chans * rows
    table = lon_table(length, modes, lat_count).transpose(1, 0, 2, 3)
    table = table.reshape(lat_count, length, lanes)
    high = table.astype(ml_dtypes.bfloat16)
    low = (table - high.astype(np.float32)).astype(ml_dtypes.bfloat16)
    back = np.ascontiguousarray(high.transpose(0, 2, 1))
    gw_rows = 4 * chans // lat_count
    copies = (4 * (all_rows // 256) + 3) * lat_count + all_rows // 128
    f32, bf16 = jnp.float32, jnp.bfloat16
    block = pltpu.VMEM((lat_count, all_rows, lanes), f32)
    modal = pltpu.VMEM((lat_len, chans, lanes), f32)
    anywhere = pl.BlockSpec(memory_space=pl.ANY)
    scalars = pl.BlockSpec(memory_space=pltpu.SMEM)
    inside = pl.BlockSpec(memory_space=pltpu.VMEM)
    mixed, gtok, gw = pl.pallas_call(
        functools.partial(band_kernel, lat_count, grp_count),
        out_shape=(
            pltpu.VMEM((all_rows, length), bf16),
            pltpu.VMEM((all_rows, length), bf16),
            pltpu.VMEM((1, gw_rows * chans), f32),
        ),
        in_specs=[anywhere] * 5 + [scalars] * 2 + [anywhere] * 4,
        out_specs=(inside, inside, inside),
        scratch_shapes=[
            pltpu.VMEM((all_rows, length), bf16),
            pltpu.VMEM((all_rows, length), bf16),
            pltpu.VMEM((lat_count, length, lanes), bf16),
            pltpu.VMEM((lat_count, length, lanes), bf16),
            pltpu.VMEM((lat_count, lanes, length), bf16),
            *[block] * 8,
            *[modal] * 4,
            pltpu.VMEM((lat_len, 8, lanes), f32),
            pltpu.VMEM((4, rows, length), f32),
            pltpu.VMEM((2, 2, rows, length), f32),
            pltpu.VMEM((2, grp_count, 2, rows, length), f32),
            *[pltpu.VMEM((2 * chans, 2 * chans), bf16)] * 4,
            *[pltpu.VMEM((chans, lanes), f32)] * 2,
            *[pltpu.VMEM((chans, 2 * chans), f32)] * 2,
            pltpu.VMEM((lat_count, gw_rows, lanes), f32),
            pltpu.VMEM((lat_count, gw_rows, lanes), f32),
            *[pltpu.VMEM(value.shape, f32) for value in (w_in, b_in, w_out, b_out)],
            pltpu.SemaphoreType.DMA((copies,)),
            pltpu.SemaphoreType.DMA((copies,)),
            pltpu.SemaphoreType.DMA((8 + lat_count,)),
        ],
        compiler_params=pltpu.CompilerParams(
            collective_id=0, has_side_effects=True, vmem_limit_bytes=56 << 20
        ),
    )(
        tokens.reshape(all_rows, length), cotangent.reshape(all_rows, length),
        jnp.asarray(high), jnp.asarray(low), jnp.asarray(back),
        gain, shift, w_in, b_in, w_out, b_out,
    )
    return (
        mixed.reshape(chans, rows, length), gtok.reshape(chans, rows, length), gw
    )


def fits(lat_count, grp_count, tokens):
    chans, rows, length = tokens.shape
    lanes = length // lat_count
    gw_rows = 4 * chans // lat_count
    return (
        lanes == 128 and lat_count & (lat_count - 1) == 0 and rows == 8
        and grp_count <= lat_count and chans % gw_rows == 0 and gw_rows % 8 == 0
        and (chans * rows) % 256 == 0 and chans % 16 == 0 and chans <= lanes
    )


def per_part(*args):
    lat_count, grp_count = lax.axis_size("lat"), lax.axis_size("grp")
    if fits(lat_count, grp_count, args[0]):
        return fused(lat_count, grp_count, *args)
    return per_device(*args)


def solution(mesh):
    in_specs = (
        P("grp", "lat", None),
        P("grp", "lat", None),
        P("grp"),
        P("grp"),
        P("grp", None, None, None),
        P("grp", None, None),
        P("grp", None, None, None),
        P("grp", None, None),
    )
    out_specs = (P("grp", "lat", None), P("grp", "lat", None), P("grp", "lat"))
    return jax.shard_map(
        per_part, mesh=mesh, in_specs=in_specs, out_specs=out_specs, check_vma=False
    )
```
